512 devices in a mesh: dp: 32 (over x, z_lo, core), tensor: 16 (over z_hi, y).
Axes of the slice: x: 4, y: 4, z: 16 (z_hi: 4, z_lo: 4; z = z_hi * 4 + z_lo), core: 2. Of those that a mesh axis runs over, the one named last changes fastest.
Arguments:
- page_patches: bfloat16 [32768, 6144], P('dp', 'tensor'), may hold values from -720 to 720
- gain: bfloat16 [6144], P('tensor'), may hold values from 0.5 to 1.5
- q_weight: bfloat16 [6144, 4096], P('dp', 'tensor'), may hold values from -0.076546554 to 0.076546554
- k_weight: bfloat16 [6144, 4096], P('dp', 'tensor'), may hold values from -2.0412415 to 2.0412415
- v_weight: bfloat16 [6144, 4096], P('dp', 'tensor'), may hold values from -0.078125 to 0.078125
- pack_lengths: int32 [32, 32], replicated, may hold values from 1 to 32, 512 in all within a row
- line_order: int32 [32, 32], replicated, may hold values from 0 to 31, each once within a row
Outputs:
- context: bfloat16 [16384, 4096], P('dp', 'tensor')
The draws below stay inside these ranges and needn't reach their ends.
Inputs may be any that keep to these rules, and one draw needn't show every extreme that they name: `pack_lengths`: every row sums to exactly 512 and holds the value 32. `line_order`: each row names every sequence 0 to 31 once.
All inputs are finite; a program needn't handle non-finite values.
Results may differ from the reference program's by a relative error of at most 0.0079.
Values may be sent and summed in bfloat16 or wider, within the bound.
No kernel may reach another device: no remote copies, remote signals or barrier semaphores. Data moves between devices by JAX's collectives and lax.ppermute only.
A program may use at most 64 MiB of HBM per device.

```python
import math
import jax
import jax.numpy as jnp
import numpy as np
from jax import lax

D = 6144
HEAD_DIM = 128
SEQ = 512
HEADS = 32
HD = 4096
MOST = 32
PAGE_DEV = 1024
PAGE_ROWS = 32768
TOKENS = 16384
N_DP = 32


def draw_page_patches(key, part):
    key_body, key_rows, key_cols = jax.random.split(jax.random.fold_in(key, 3), 3)
    row_scale = jnp.exp(jax.random.uniform(key_rows, (PAGE_ROWS, 1), jnp.float32, 0.0, math.log(10.0)))
    ramp = math.log(3.0) * jnp.arange(D, dtype=jnp.float32)[None, :] / D
    col_scale = jnp.exp(jax.random.uniform(key_cols, (1, D), jnp.float32, 0.0, math.log(4.0)) + ramp)
    entries = jnp.clip(jax.random.normal(key_body, (PAGE_ROWS, D), jnp.float32), -6.0, 6.0)
    return (entries * row_scale * col_scale).astype(jnp.bfloat16)


def projection_pair(key):
    key_base, key_noise = jax.random.split(jax.random.fold_in(key, 11), 2)
    spread = D ** (-0.5)
    query_base = jnp.clip(jax.random.normal(key_base, (D, HD), jnp.float32), -6.0, 6.0) * spread
    partner = jnp.clip(jax.random.normal(key_noise, (D, HD), jnp.float32), -6.0, 6.0) * spread
    return (query_base, partner)


def draw_q_weight(key, part):
    return projection_pair(key)[0].astype(jnp.bfloat16)


def draw_k_weight(key, part):
    return projection_pair(key)[1].astype(jnp.bfloat16)


def block_scale(rng, shape, cuts, smallest, high):
    level, own = 1.0, jax.random.fold_in(rng, 6)
    for dim, parts in cuts:
        heights = jnp.exp(jax.random.uniform(jax.random.fold_in(own, dim), (parts,), jnp.float32, smallest / len(cuts), high / len(cuts)))
        level = level * jnp.repeat(heights, shape[dim] // parts).reshape([-1 if axis == dim else 1 for axis in range(len(shape))])
    return level


def split_up(amount, total, limit, lean):
    weights = [(1 << 20) // math.isqrt(standing ** lean) + 1 for standing in range(2, amount + 1)]
    surplus, given = total - limit - (amount - 1), [1] * (amount - 1)
    while surplus > 0:
        movable = [i for i in range(amount - 1) if given[i] < limit]
        whole, budget = sum([weights[i] for i in movable]), surplus
        for i in movable:
            more = min(limit - given[i], max(1, budget * weights[i] // whole), surplus)
            given[i] = given[i] + more
            surplus = surplus - more
    return np.array([limit] + given)


def uneven_parts(key, count, total, bound, skew):
    if count == 2:
        one = jax.random.randint(key, (), max(1, total - bound), min(bound, total - 1) + 1)
        return jnp.stack([one, total - one])
    sizes = jnp.asarray(split_up(count, total, bound, skew), jnp.int32)
    couples = (count - 1) // 2
    giver, receiver = sizes[1:1 + 2 * couples:2], sizes[2:2 + 2 * couples:2]
    room = jnp.minimum(giver - 1, bound - receiver)
    passed = jax.random.randint(jax.random.fold_in(key, 1), (couples,), 0, 1 << 20) % (room + 1)
    sizes = sizes.at[1:1 + 2 * couples:2].set(giver - passed).at[2:2 + 2 * couples:2].set(receiver + passed)
    return sizes[jax.random.permutation(jax.random.fold_in(key, 2), count)]


def gaussian(rng, extent, deviation, bound, cuts=(), kind=jnp.bfloat16):
    array = jax.random.normal(rng, extent, jnp.float32) * deviation
    if len(cuts) > 0:
        array = block_scale(rng, extent, cuts, -0.22, 0.18) * array
    return jnp.clip(array, min=-bound, max=bound).astype(kind)


def setup_inputs(seed: int = 0) -> dict:
    seeds = jax.random.split(jax.random.key(seed), 8)
    return {
        "page_patches": draw_page_patches(jax.random.fold_in(seeds[7], 71), 0),
        "gain": jnp.clip(1.0 + 0.1 * jax.random.normal(seeds[1], (D,), jnp.float32), 0.5, 1.5).astype(jnp.bfloat16),
        "q_weight": draw_q_weight(jax.random.fold_in(seeds[7], 71), 0),
        "k_weight": draw_k_weight(jax.random.fold_in(seeds[7], 71), 0),
        "v_weight": gaussian(seeds[4], (D, HD), D ** -0.5, 0.078125, ((0, 32), (1, 16))),
        "pack_lengths": jax.vmap(lambda own: uneven_parts(own, N_DP, SEQ, MOST, 2))(jax.random.split(seeds[5], N_DP)).reshape((N_DP, N_DP)).astype(jnp.int32),
        "line_order": jax.vmap(lambda own: jax.random.permutation(own, N_DP))(jax.random.split(seeds[6], N_DP)).reshape((N_DP, N_DP)).astype(jnp.int32),
    }


norm_epsilon = 1e-06

def packing_rows(pack_lengths, line_order):
    line_ends = jnp.cumsum(pack_lengths, axis=1).astype(jnp.int32)
    line_starts = (line_ends - pack_lengths).astype(jnp.int32)
    places = jnp.arange(SEQ, dtype=jnp.int32)
    targets = jnp.arange(N_DP, dtype=jnp.int32)
    segment = lax.optimization_barrier(jnp.sum((line_ends[:, None, :] <= places[None, :, None]).astype(jnp.int32), axis=2)).astype(jnp.int32)
    offset = (places[None, :] - jnp.take_along_axis(line_starts, segment, axis=1)).astype(jnp.int32)
    slot_of = lax.optimization_barrier(jnp.sum(jnp.where(line_order[:, :, None] == targets[None, None, :], targets[None, :, None], 0), axis=1)).astype(jnp.int32)
    slot_index = slot_of[segment, targets[:, None]].astype(jnp.int32)
    source_rows = (segment * PAGE_DEV + slot_index * MOST + offset).astype(jnp.int32)
    return (source_rows, segment)

def attend(queries, keys, values, segment):
    query_heads = queries.reshape(SEQ, HEADS, HEAD_DIM).astype(jnp.float32)
    key_heads = keys.reshape(SEQ, HEADS, HEAD_DIM).astype(jnp.float32)
    value_heads = values.reshape(SEQ, HEADS, HEAD_DIM).astype(jnp.float32)
    scores = jnp.einsum('qhd,khd->hqk', query_heads, key_heads) * (1.0 / math.sqrt(HEAD_DIM))
    same_line = segment[:, None] == segment[None, :]
    scores = jnp.where(same_line[None, :, :], scores, -jnp.inf)
    row_max = lax.optimization_barrier(jnp.max(scores, axis=2, keepdims=True))
    expo = jnp.exp(scores - row_max)
    attn_probs = (expo / lax.optimization_barrier(jnp.sum(expo, axis=2, keepdims=True))).astype(jnp.bfloat16)
    context = jnp.einsum('hqk,khd->qhd', attn_probs.astype(jnp.float32), value_heads)
    return context.astype(jnp.bfloat16).reshape(SEQ, HD)

def reference(page_patches, gain, q_weight, k_weight, v_weight, pack_lengths, line_order):
    source_rows, segment = packing_rows(pack_lengths, line_order)

    def one_sequence(inputs):
        row_ids, line_ids = inputs
        packed = jnp.take(page_patches, row_ids, axis=0).astype(jnp.float32)
        row_mean = lax.optimization_barrier(jnp.mean(packed, axis=1, keepdims=True))
        row_var = lax.optimization_barrier(jnp.mean(jnp.square(packed - row_mean), axis=1, keepdims=True))
        normed = ((packed - row_mean) * lax.rsqrt(row_var + norm_epsilon) * gain.astype(jnp.float32)).astype(jnp.bfloat16)
        queries = jnp.dot(normed, q_weight, preferred_element_type=jnp.float32).astype(jnp.bfloat16)
        keys = jnp.dot(normed, k_weight, preferred_element_type=jnp.float32).astype(jnp.bfloat16)
        values = jnp.dot(normed, v_weight, preferred_element_type=jnp.float32).astype(jnp.bfloat16)
        return attend(queries, keys, values, line_ids)
    contexts = lax.map(one_sequence, (source_rows, segment))
    return contexts.reshape(TOKENS, HD)
```

```python
import math

import jax
import jax.numpy as jnp
from jax import lax
from jax.experimental import pallas as pl
from jax.experimental.pallas import tpu as pltpu
from jax.sharding import PartitionSpec as P

HEAD_DIM = 128
NORM_EPSILON = 1e-06
Z_PARTS, Y_PARTS = 4, 4
GAIN_ROWS = 16
ROW_TILE = 16


def z_shift(step):
    return [
        (z * Y_PARTS + y, (z + step) % Z_PARTS * Y_PARTS + y)
        for z in range(Z_PARTS)
        for y in range(Y_PARTS)
    ]


def y_shift(step):
    return [
        (z * Y_PARTS + y, z * Y_PARTS + (y + step) % Y_PARTS)
        for z in range(Z_PARTS)
        for y in range(Y_PARTS)
    ]


def both_ways(block, shift, cut):
    up = lax.ppermute(block, "tensor", shift(1))
    down = lax.ppermute(block, "tensor", shift(-1))
    far_top = lax.ppermute(up[:cut], "tensor", shift(1))
    far_rest = lax.ppermute(down[cut:], "tensor", shift(-1))
    return up, down, far_top, far_rest


def attend_kernel(slots, count, rows, cut, *refs):
    places_ref, blocks = refs[0], refs[1 : 1 + count]
    weight_ref, seg_col_ref, seg_row_ref, out_ref, normed_ref = refs[1 + count :]
    features = normed_ref.shape[1]
    width = blocks[0].shape[1]

    def part(pieces, row):
        for ref_index, ref_row, first, last in pieces:
            if first <= row < last:
                return blocks[ref_index], ref_row - first
        return None

    gains = []
    for pieces in slots:
        ref, shift = part(pieces, rows)
        gains.append(ref[pl.ds(rows + shift, GAIN_ROWS), :][:1].astype(jnp.float32))
    columns = [pl.ds(pl.multiple_of(places_ref[j] * width, 128), width) for j in range(len(slots))]

    for first, last in ((0, cut), (cut, rows)):
        sources = [part(pieces, first) for pieces in slots]

        def step(i, carry):
            row = first + i * ROW_TILE
            def load(j):
                ref, shift = sources[j]
                at = pl.multiple_of(row + shift, ROW_TILE)
                return ref[pl.ds(at, ROW_TILE), :].astype(jnp.float32)

            total = load(0)
            for j in range(1, len(slots)):
                total = total + load(j)
            mean = jnp.sum(total, axis=1, keepdims=True) * (1.0 / features)
            square = jnp.square(load(0) - mean)
            for j in range(1, len(slots)):
                square = square + jnp.square(load(j) - mean)
            var = jnp.sum(square, axis=1, keepdims=True) * (1.0 / features)
            scale = lax.rsqrt(var + NORM_EPSILON)
            at = pl.multiple_of(row, ROW_TILE)
            for j in range(len(slots)):
                normed_ref[pl.ds(at, ROW_TILE), columns[j]] = (
                    (load(j) - mean) * scale * gains[j]
                ).astype(jnp.bfloat16)
            return carry

        lax.fori_loop(0, (last - first) // ROW_TILE, step, 0)

    local = out_ref.shape[1]
    sums = jnp.dot(normed_ref[...], weight_ref[...], preferred_element_type=jnp.float32)
    sums = sums.astype(jnp.bfloat16)
    query, key, value = sums[:, :local], sums[:, local : 2 * local], sums[:, 2 * local :]
    span, window = 128, 256
    for row in range(0, rows, span):
        low = min(max(row - (window - span) // 2, 0), rows - window)
        same = seg_col_ref[row : row + span, :1] == seg_row_ref[:1, low : low + window]
        for col in range(0, local, HEAD_DIM):
            head = slice(col, col + HEAD_DIM)
            scores = lax.dot_general(
                query[row : row + span, head],
                key[low : low + window, head],
                (((1,), (1,)), ((), ())),
                preferred_element_type=jnp.float32,
            ) * (1.0 / math.sqrt(HEAD_DIM))
            scores = jnp.where(same, scores, -jnp.inf)
            expo = jnp.exp(scores - jnp.max(scores, axis=1, keepdims=True))
            probs = (expo / jnp.sum(expo, axis=1, keepdims=True)).astype(jnp.bfloat16)
            out_ref[row : row + span, head] = jnp.dot(
                probs, value[low : low + window, head], preferred_element_type=jnp.float32
            ).astype(jnp.bfloat16)


def shards(page_patches, gain, q_weight, k_weight, v_weight, pack_lengths, line_order):
    groups = lax.axis_size("dp")
    page_index = lax.axis_index("dp")
    width = page_patches.shape[1]
    slot_rows = page_patches.shape[0] // groups
    rows = slot_rows * groups // 2
    local = q_weight.shape[1]
    weights = lax.all_gather(
        jnp.concatenate([q_weight, k_weight, v_weight], axis=1), "dp", axis=0, tiled=True
    )
    targets = jnp.arange(groups, dtype=jnp.int32)
    my_order = lax.dynamic_index_in_dim(line_order, page_index, 0, keepdims=False)
    slot_for = jnp.sum(
        jnp.where(my_order[None, :] == targets[:, None], targets[None, :], 0), axis=1
    )
    slots = page_patches.reshape(groups, slot_rows, width)
    outgoing = jnp.take(slots, slot_for, axis=0)
    incoming = lax.all_to_all(outgoing, "dp", split_axis=0, concat_axis=0, tiled=True)
    my_lengths = lax.dynamic_index_in_dim(pack_lengths, page_index, 0, keepdims=False)
    line_ends = jnp.cumsum(my_lengths)
    line_starts = line_ends - my_lengths
    row_ids = jnp.arange(rows, dtype=jnp.int32)
    segment = jnp.sum((line_ends[None, :] <= row_ids[:, None]).astype(jnp.int32), axis=1)
    start_of_row = jnp.sum(
        jnp.where(segment[:, None] == targets[None, :], line_starts[None, :], 0), axis=1
    )
    source_rows = segment * slot_rows + row_ids - start_of_row
    packed = jnp.take(incoming.reshape(groups * slot_rows, width), source_rows, axis=0)

    own = jnp.concatenate([packed, jnp.broadcast_to(gain[None, :], (GAIN_ROWS, width))], axis=0)
    all_rows = rows + GAIN_ROWS
    cut = rows // 2 + GAIN_ROWS
    z_up, z_down, z_far_top, z_far_rest = both_ways(own, z_shift, cut)
    pair = jnp.concatenate([z_up, z_down], axis=0)
    far = jnp.concatenate([z_far_top, z_far_rest], axis=0)
    blocks, slot_list, shifts = [], [], []

    def add(array):
        blocks.append(array)
        return len(blocks) - 1

    def slot(dz, dy, *pieces):
        slot_list.append(pieces)
        shifts.append((dz, dy))

    for array, dzs in ((own, (0,)), (pair, (-1, 1)), (far, (2,))):
        half = cut if len(dzs) == 1 else all_rows
        up, down, far_top, far_rest = both_ways(array, y_shift, half)
        for dy, source in ((0, array), (-1, up), (1, down)):
            ref = add(source)
            for k, dz in enumerate(dzs):
                slot(dz, dy, (ref, k * all_rows, 0, all_rows))
        top, rest = add(far_top), add(far_rest)
        if len(dzs) == 1:
            slot(dzs[0], 2, (top, 0, 0, cut), (rest, 0, cut, all_rows))
        else:
            slot(dzs[0], 2, (top, 0, 0, all_rows))
            slot(dzs[1], 2, (rest, 0, 0, all_rows))
    tensor = lax.axis_index("tensor")
    my_z, my_y = tensor // Y_PARTS, tensor % Y_PARTS
    step_z = jnp.array([dz for dz, _ in shifts], jnp.int32)
    step_y = jnp.array([dy for _, dy in shifts], jnp.int32)
    places = (my_z + step_z + Z_PARTS) % Z_PARTS * Y_PARTS + (my_y + step_y + Y_PARTS) % Y_PARTS

    def kernel(*refs):
        attend_kernel(slot_list, len(blocks), rows, cut, *refs)

    vmem = pl.BlockSpec(memory_space=pltpu.VMEM)
    return pl.pallas_call(
        kernel,
        out_shape=jax.ShapeDtypeStruct((rows, local), jnp.bfloat16),
        in_specs=[pl.BlockSpec(memory_space=pltpu.SMEM)] + [vmem] * (len(blocks) + 3),
        out_specs=vmem,
        scratch_shapes=[pltpu.VMEM((rows, width * len(slot_list)), jnp.bfloat16)],
        name="norm_project_attend",
    )(places, *blocks, weights, segment[:, None], segment[None, :])


def solution(mesh):
    return jax.shard_map(
        shards,
        mesh=mesh,
        in_specs=(
            P("dp", "tensor"),
            P("tensor"),
            P("dp", "tensor"),
            P("dp", "tensor"),
            P("dp", "tensor"),
            P(),
            P(),
        ),
        out_specs=P("dp", "tensor"),
        check_vma=False,
    )
```

```python
import math

import jax
import jax.numpy as jnp
from jax import lax
from jax.experimental import pallas as pl
from jax.experimental.pallas import tpu as pltpu
from jax.sharding import PartitionSpec as P

HEAD_DIM = 128
NORM_EPSILON = 1e-06
Z_PARTS, Y_PARTS = 4, 4
GAIN_ROWS = 16
ROW_TILE = 16


def z_shift(step):
    return [
        (z * Y_PARTS + y, (z + step) % Z_PARTS * Y_PARTS + y)
        for z in range(Z_PARTS)
        for y in range(Y_PARTS)
    ]


def y_shift(step):
    return [
        (z * Y_PARTS + y, z * Y_PARTS + (y + step) % Y_PARTS)
        for z in range(Z_PARTS)
        for y in range(Y_PARTS)
    ]


def dp_move(x_step, z_step, core_step):
    pairs = []
    for x in range(4):
        for z in range(4):
            for core in range(2):
                to = (x + x_step) % 4 * 8 + (z + z_step) % 4 * 2 + (core + core_step) % 2
                pairs.append((x * 8 + z * 2 + core, to))
    return pairs


def attend_kernel(slots, count, rows, cut, strip, *refs):
    places_ref, strips_ref, blocks = refs[0], refs[1], refs[2 : 2 + count]
    held_ref, swapped_ref, seg_col_ref, seg_row_ref, out_ref = refs[2 + count : 7 + count]
    normed_ref, weight_ref, weight_sem = refs[7 + count :]
    features = normed_ref.shape[1]
    width = blocks[0].shape[1]
    copies = []
    for source, ref in enumerate((held_ref, swapped_ref)):
        for k in range(ref.shape[0] // strip):
            at = pl.multiple_of(strips_ref[source * (ref.shape[0] // strip) + k] * strip, 16)
            copies.append(
                pltpu.make_async_copy(
                    ref.at[pl.ds(k * strip, strip), :],
                    weight_ref.at[pl.ds(at, strip), :],
                    weight_sem,
                )
            )
    for copy in copies:
        copy.start()


    def part(pieces, row):
        for ref, start, first, last in pieces:
            if first <= row < last:
                return blocks[ref], start - first

    gains = []
    for pieces in slots:
        ref, shift = part(pieces, rows)
        gains.append(ref[pl.ds(rows + shift, GAIN_ROWS), :][:1].astype(jnp.float32))
    columns = [pl.ds(pl.multiple_of(places_ref[j] * width, 128), width) for j in range(len(slots))]

    for first, last in ((0, cut), (cut, rows)):
        sources = [part(pieces, first) for pieces in slots]

        def step(i, carry):
            at = pl.multiple_of(first + i * ROW_TILE, ROW_TILE)

            def load(j):
                ref, shift = sources[j]
                return ref[pl.ds(at + shift, ROW_TILE), :].astype(jnp.float32)

            total = load(0)
            for j in range(1, len(slots)):
                total = total + load(j)
            mean = jnp.sum(total, axis=1, keepdims=True) * (1.0 / features)
            square = jnp.square(load(0) - mean)
            for j in range(1, len(slots)):
                square = square + jnp.square(load(j) - mean)
            var = jnp.sum(square, axis=1, keepdims=True) * (1.0 / features)
            scale = lax.rsqrt(var + NORM_EPSILON)
            for j in range(len(slots)):
                normed_ref[pl.ds(at, ROW_TILE), columns[j]] = (
                    (load(j) - mean) * scale * gains[j]
                ).astype(jnp.bfloat16)
            return carry

        lax.fori_loop(0, (last - first) // ROW_TILE, step, 0)
    for copy in copies:
        copy.wait()
    local = out_ref.shape[1]
    sums = jnp.dot(normed_ref[...], weight_ref[...], preferred_element_type=jnp.float32)
    sums = sums.astype(jnp.bfloat16)
    query, key, value = sums[:, :local], sums[:, local : 2 * local], sums[:, 2 * local :]
    span, window = 128, 256
    for row in range(0, rows, span):
        low = min(max(row - (window - span) // 2, 0), rows - window)
        same = seg_col_ref[row : row + span, :1] == seg_row_ref[:1, low : low + window]
        for col in range(0, local, HEAD_DIM):
            head = slice(col, col + HEAD_DIM)
            scores = lax.dot_general(
                query[row : row + span, head],
                key[low : low + window, head],
                (((1,), (1,)), ((), ())),
                preferred_element_type=jnp.float32,
            ) * (1.0 / math.sqrt(HEAD_DIM))
            scores = jnp.where(same, scores, -jnp.inf)
            expo = jnp.exp(scores - jnp.max(scores, axis=1, keepdims=True))
            probs = (expo / jnp.sum(expo, axis=1, keepdims=True)).astype(jnp.bfloat16)
            out_ref[row : row + span, head] = jnp.dot(
                probs, value[low : low + window, head], preferred_element_type=jnp.float32
            ).astype(jnp.bfloat16)


def shards(page_patches, gain, q_weight, k_weight, v_weight, pack_lengths, line_order):
    groups = lax.axis_size("dp")
    page_index = lax.axis_index("dp")
    width = page_patches.shape[1]
    slot_rows = page_patches.shape[0] // groups
    rows = slot_rows * groups // 2
    local = q_weight.shape[1]
    strip = q_weight.shape[0]
    weight = jnp.concatenate([q_weight, k_weight, v_weight], axis=1)
    column = [lax.ppermute(weight, "dp", dp_move(0, k, 0)) for k in (1, 2, 3)]
    targets = jnp.arange(groups, dtype=jnp.int32)
    my_order = lax.dynamic_index_in_dim(line_order, page_index, 0, keepdims=False)
    slot_for = jnp.sum(
        jnp.where(my_order[None, :] == targets[:, None], targets[None, :], 0), axis=1
    )
    slots = page_patches.reshape(groups, slot_rows, width)
    outgoing = jnp.take(slots, slot_for, axis=0)
    incoming = lax.all_to_all(outgoing, "dp", split_axis=0, concat_axis=0, tiled=True)
    incoming, *column = lax.optimization_barrier((incoming, *column))
    column = jnp.concatenate([weight] + column, axis=0)
    my_lengths = lax.dynamic_index_in_dim(pack_lengths, page_index, 0, keepdims=False)
    line_ends = jnp.cumsum(my_lengths)
    line_starts = line_ends - my_lengths
    row_ids = jnp.arange(rows, dtype=jnp.int32)
    segment = jnp.sum((line_ends[None, :] <= row_ids[:, None]).astype(jnp.int32), axis=1)
    start_of_row = jnp.sum(
        jnp.where(segment[:, None] == targets[None, :], line_starts[None, :], 0), axis=1
    )
    source_rows = segment * slot_rows + row_ids - start_of_row
    packed = jnp.take(incoming.reshape(groups * slot_rows, width), source_rows, axis=0)

    own = jnp.concatenate([packed, jnp.broadcast_to(gain[None, :], (GAIN_ROWS, width))], axis=0)
    all_rows = rows + GAIN_ROWS
    cut = rows // 2 + GAIN_ROWS
    z_up, z_down = (lax.ppermute(own, "tensor", z_shift(k)) for k in (1, -1))
    x_up, x_down = (lax.ppermute(column, "dp", dp_move(k, 0, 0)) for k in (1, 3))
    own_up = lax.ppermute(own, "tensor", y_shift(1))
    own_up, own_again = lax.optimization_barrier((own_up, own))
    own_down = lax.ppermute(own_again, "tensor", y_shift(-1))
    z_up, z_down, own_up, own_down, x_up, x_down = lax.optimization_barrier(
        (z_up, z_down, own_up, own_down, x_up, x_down)
    )
    z_far = [
        lax.ppermute(z_up[:cut], "tensor", z_shift(1)),
        lax.ppermute(z_down[cut:], "tensor", z_shift(-1)),
    ]
    pair = jnp.concatenate([z_up, z_down], axis=0)
    pair_up, pair_down = (lax.ppermute(pair, "tensor", y_shift(k)) for k in (1, -1))
    x_far = lax.ppermute(column, "dp", dp_move(2, 0, 0))
    *z_far, pair_up, pair_down, x_far = lax.optimization_barrier(
        (*z_far, pair_up, pair_down, x_far)
    )
    far = jnp.concatenate(z_far, axis=0)
    far_y = [lax.ppermute(far, "tensor", y_shift(k)) for k in (1, -1, 2)]
    far_up = jnp.concatenate([pair_up[:all_rows], own_up[:cut]], axis=0)
    far_down = jnp.concatenate([pair_down[all_rows:], own_down[cut:]], axis=0)
    far_up = lax.ppermute(far_up, "tensor", y_shift(1))
    far_down = lax.ppermute(far_down, "tensor", y_shift(-1))
    held = jnp.concatenate([column, x_up, x_far, x_down], axis=0)
    swapped = lax.ppermute(held, "dp", dp_move(0, 0, 1))

    blocks = [own, own_up, own_down, pair, pair_up, pair_down, far_up, far_down, far, *far_y]
    whole = lambda ref, row: ((ref, row, 0, all_rows),)
    slots_at = [
        ((0, 0), whole(0, 0)),
        ((0, -1), whole(1, 0)),
        ((0, 1), whole(2, 0)),
        ((0, 2), ((6, all_rows, 0, cut), (7, all_rows, cut, all_rows))),
        ((-1, 0), whole(3, 0)),
        ((1, 0), whole(3, all_rows)),
        ((-1, -1), whole(4, 0)),
        ((1, -1), whole(4, all_rows)),
        ((-1, 1), whole(5, 0)),
        ((1, 1), whole(5, all_rows)),
        ((-1, 2), whole(6, 0)),
        ((1, 2), whole(7, 0)),
        ((2, 0), whole(8, 0)),
        ((2, -1), whole(9, 0)),
        ((2, 1), whole(10, 0)),
        ((2, 2), whole(11, 0)),
    ]
    shifts, slots_at = zip(*slots_at)
    tensor = lax.axis_index("tensor")
    my_z, my_y = tensor // Y_PARTS, tensor % Y_PARTS
    step_z = jnp.array([dz for dz, _ in shifts], jnp.int32)
    step_y = jnp.array([dy for _, dy in shifts], jnp.int32)
    places = (my_z + step_z + Z_PARTS) % Z_PARTS * Y_PARTS + (my_y + step_y + Y_PARTS) % Y_PARTS

    my_x, my_lo, my_core = page_index // 8, page_index // 2 % 4, page_index % 2
    k = jnp.arange(groups, dtype=jnp.int32)
    step_core, step_x, step_lo = k // 16, k // 4 % 4, k % 4
    strips = (my_x - step_x + 4) % 4 * 8 + (my_lo - step_lo + 4) % 4 * 2 + (my_core + step_core) % 2

    def kernel(*refs):
        attend_kernel(slots_at, len(blocks), rows, cut, strip, *refs)

    features = width * len(slots_at)
    vmem = pl.BlockSpec(memory_space=pltpu.VMEM)
    smem, hbm = pl.BlockSpec(memory_space=pltpu.SMEM), pl.BlockSpec(memory_space=pl.ANY)
    return pl.pallas_call(
        kernel,
        out_shape=jax.ShapeDtypeStruct((rows, local), jnp.bfloat16),
        in_specs=[smem, smem] + [vmem] * len(blocks) + [hbm, hbm, vmem, vmem],
        out_specs=vmem,
        scratch_shapes=[
            pltpu.VMEM((rows, features), jnp.bfloat16),
            pltpu.VMEM((features, 3 * local), jnp.bfloat16),
            pltpu.SemaphoreType.DMA,
        ],
        name="norm_project_attend",
    )(places, strips, *blocks, held, swapped, segment[:, None], segment[None, :])


def solution(mesh):
    return jax.shard_map(
        shards,
        mesh=mesh,
        in_specs=(
            P("dp", "tensor"),
            P("tensor"),
            P("dp", "tensor"),
            P("dp", "tensor"),
            P("dp", "tensor"),
            P(),
            P(),
        ),
        out_specs=P("dp", "tensor"),
        check_vma=False,
    )
```

```python
import math

import jax
import jax.numpy as jnp
from jax import lax
from jax.experimental import pallas as pl
from jax.experimental.pallas import tpu as pltpu
from jax.sharding import PartitionSpec as P

HEAD_DIM = 128
NORM_EPSILON = 1e-06
Z_PARTS, Y_PARTS = 4, 4
GAIN_ROWS = 16
ROW_TILE = 16


def z_shift(step):
    return [
        (z * Y_PARTS + y, (z + step) % Z_PARTS * Y_PARTS + y)
        for z in range(Z_PARTS)
        for y in range(Y_PARTS)
    ]


def y_shift(step):
    return [
        (z * Y_PARTS + y, z * Y_PARTS + (y + step) % Y_PARTS)
        for z in range(Z_PARTS)
        for y in range(Y_PARTS)
    ]


def dp_groups(varying):
    groups = {}
    for x in range(4):
        for z in range(4):
            for core in range(2):
                key = tuple(v for name, v in (("x", x), ("z", z), ("c", core)) if name not in varying)
                groups.setdefault(key, []).append(x * 8 + z * 2 + core)
    return list(groups.values())


def load_weights(source_ref, weight_ref, sem, strip):
    copies = []
    for x in range(4):
        for z in range(4):
            for core in range(2):
                held, wanted = (x * 2 + core) * 4 + z, x * 8 + z * 2 + core
                copies.append(
                    pltpu.make_async_copy(
                        source_ref.at[pl.ds(held * strip, strip), :],
                        weight_ref.at[pl.ds(wanted * strip, strip), :],
                        sem,
                    )
                )
    for copy in copies:
        copy.start()
    return copies


def slot_columns(places_ref, count, width):
    return [pl.ds(pl.multiple_of(places_ref[j] * width, 128), width) for j in range(count)]


def normalize(sources, gains, columns, rows, normed_ref):
    features = normed_ref.shape[1]

    def step(i, carry):
        at = pl.multiple_of(i * ROW_TILE, ROW_TILE)

        def load(j):
            ref, start = sources[j]
            return ref[pl.ds(at + start, ROW_TILE), :].astype(jnp.float32)

        total = load(0)
        for j in range(1, len(sources)):
            total = total + load(j)
        mean = jnp.sum(total, axis=1, keepdims=True) * (1.0 / features)
        square = jnp.square(load(0) - mean)
        for j in range(1, len(sources)):
            square = square + jnp.square(load(j) - mean)
        var = jnp.sum(square, axis=1, keepdims=True) * (1.0 / features)
        scale = lax.rsqrt(var + NORM_EPSILON)
        for j in range(len(sources)):
            normed_ref[pl.ds(at, ROW_TILE), columns[j]] = (
                (load(j) - mean) * scale * gains[j]
            ).astype(jnp.bfloat16)
        return carry

    lax.fori_loop(0, rows // ROW_TILE, step, 0)


def first_half_kernel(slots, count, strip, *refs):
    places_ref, blocks = refs[0], refs[1 : 1 + count]
    source_ref, sums_ref, gain_ref, normed_ref, weight_ref, sem = refs[1 + count :]
    copies = load_weights(source_ref, weight_ref, sem, strip)
    columns = slot_columns(places_ref, len(slots), blocks[0].shape[1])
    gains = []
    for column, (ref, start) in zip(columns, slots):
        gain = blocks[ref][pl.ds(start - GAIN_ROWS, GAIN_ROWS), :][:1].astype(jnp.float32)
        gain_ref[:, column] = gain
        gains.append(gain)
    sources = [(blocks[ref], start) for ref, start in slots]
    normalize(sources, gains, columns, normed_ref.shape[0], normed_ref)
    for copy in copies:
        copy.wait()
    sums_ref[...] = jnp.dot(
        normed_ref[...], weight_ref[...], preferred_element_type=jnp.float32
    ).astype(jnp.bfloat16)


def second_half_kernel(slots, count, strip, *refs):
    places_ref, blocks = refs[0], refs[1 : 1 + count]
    source_ref, first_ref, gain_ref, seg_col_ref, seg_row_ref, out_ref = refs[1 + count : 7 + count]
    normed_ref, weight_ref, sums_ref, sem = refs[7 + count :]
    copies = load_weights(source_ref, weight_ref, sem, strip)
    columns = slot_columns(places_ref, len(slots), blocks[0].shape[1])
    gains = [gain_ref[:, column] for column in columns]
    sources = [(blocks[ref], start) for ref, start in slots]
    half = normed_ref.shape[0]
    normalize(sources, gains, columns, half, normed_ref)
    sums_ref[:half] = first_ref[...]
    for copy in copies:
        copy.wait()
    sums_ref[half:] = jnp.dot(
        normed_ref[...], weight_ref[...], preferred_element_type=jnp.float32
    ).astype(jnp.bfloat16)
    rows, local = out_ref.shape
    span, window = 128, 256
    for row in range(0, rows, span):
        low = min(max(row - (window - span) // 2, 0), rows - window)
        same = seg_col_ref[row : row + span, :1] == seg_row_ref[:1, low : low + window]
        for col in range(0, local, HEAD_DIM):
            query = sums_ref[row : row + span, col : col + HEAD_DIM]
            key = sums_ref[low : low + window, local + col : local + col + HEAD_DIM]
            value = sums_ref[low : low + window, 2 * local + col : 2 * local + col + HEAD_DIM]
            scores = lax.dot_general(
                query, key, (((1,), (1,)), ((), ())), preferred_element_type=jnp.float32
            ) * (1.0 / math.sqrt(HEAD_DIM))
            scores = jnp.where(same, scores, -jnp.inf)
            expo = jnp.exp(scores - jnp.max(scores, axis=1, keepdims=True))
            probs = (expo / jnp.sum(expo, axis=1, keepdims=True)).astype(jnp.bfloat16)
            out_ref[row : row + span, col : col + HEAD_DIM] = jnp.dot(
                probs, value, preferred_element_type=jnp.float32
            ).astype(jnp.bfloat16)


def along_y(block, last):
    return [lax.ppermute(block, "tensor", y_shift(step)) for step in (2, -1, 1)] + last


def shards(page_patches, gain, q_weight, k_weight, v_weight, pack_lengths, line_order):
    groups = lax.axis_size("dp")
    page_index = lax.axis_index("dp")
    width = page_patches.shape[1]
    slot_rows = page_patches.shape[0] // groups
    rows = slot_rows * groups // 2
    half = rows // 2
    local = q_weight.shape[1]
    strip = q_weight.shape[0]
    weight = jnp.concatenate([q_weight, k_weight, v_weight], axis=1)
    for varying in ("z", "xc"):
        weight = lax.all_gather(
            weight, "dp", axis=0, tiled=True, axis_index_groups=dp_groups(varying)
        )
    targets = jnp.arange(groups, dtype=jnp.int32)
    my_order = lax.dynamic_index_in_dim(line_order, page_index, 0, keepdims=False)
    slot_for = jnp.sum(
        jnp.where(my_order[None, :] == targets[:, None], targets[None, :], 0), axis=1
    )
    slots = page_patches.reshape(groups, slot_rows, width)
    outgoing = jnp.take(slots, slot_for, axis=0)
    incoming = lax.all_to_all(outgoing, "dp", split_axis=0, concat_axis=0, tiled=True)
    my_lengths = lax.dynamic_index_in_dim(pack_lengths, page_index, 0, keepdims=False)
    line_ends = jnp.cumsum(my_lengths)
    line_starts = line_ends - my_lengths
    row_ids = jnp.arange(rows, dtype=jnp.int32)
    segment = jnp.sum((line_ends[None, :] <= row_ids[:, None]).astype(jnp.int32), axis=1)
    start_of_row = jnp.sum(
        jnp.where(segment[:, None] == targets[None, :], line_starts[None, :], 0), axis=1
    )
    source_rows = segment * slot_rows + row_ids - start_of_row
    packed = jnp.take(incoming.reshape(groups * slot_rows, width), source_rows, axis=0)

    gain_rows = jnp.broadcast_to(gain[None, :], (GAIN_ROWS, width))
    own = jnp.concatenate([gain_rows, packed], axis=0)
    top, rest = own[: half + GAIN_ROWS], own[half + GAIN_ROWS :]

    up, down = z_shift(1), z_shift(-1)
    *own_y, top_down, top_up, rest = lax.optimization_barrier(
        (
            *along_y(own, []),
            lax.ppermute(top, "tensor", down),
            lax.ppermute(top, "tensor", up),
            rest,
        )
    )
    pair = jnp.concatenate([top_up, top_down], axis=0)
    *pair_y, rest_down, top_far, rest = lax.optimization_barrier(
        (
            *along_y(pair, []),
            lax.ppermute(rest, "tensor", down),
            lax.ppermute(top_up, "tensor", up),
            rest,
        )
    )
    *far_y, rest_far, rest_up = lax.optimization_barrier(
        (
            *along_y(top_far, []),
            lax.ppermute(rest_down, "tensor", down),
            lax.ppermute(rest, "tensor", up),
        )
    )
    trio = jnp.concatenate([rest_up, rest_down, rest_far], axis=0)
    trio_y = along_y(trio, [])

    shifts = [(dz, dy) for dy in (2, 1, -1, 0) for dz in (0, -1, 1, 2)]
    tensor = lax.axis_index("tensor")
    my_z, my_y = tensor // Y_PARTS, tensor % Y_PARTS
    step_z = jnp.array([dz for dz, _ in shifts], jnp.int32)
    step_y = jnp.array([dy for _, dy in shifts], jnp.int32)
    places = (my_z + step_z + Z_PARTS) % Z_PARTS * Y_PARTS + (my_y + step_y + Y_PARTS) % Y_PARTS

    first_blocks, first_slots, second_blocks, second_slots = [], [], [], []
    for k, arrays in enumerate(zip(own_y + [own], pair_y + [pair], far_y + [top_far])):
        first_blocks += arrays
        first_slots += [
            (3 * k, GAIN_ROWS),
            (3 * k + 1, GAIN_ROWS),
            (3 * k + 1, half + 2 * GAIN_ROWS),
            (3 * k + 2, GAIN_ROWS),
        ]
    for k, arrays in enumerate(zip(own_y + [own], trio_y + [trio])):
        second_blocks += arrays
        second_slots += [(2 * k, half + GAIN_ROWS)] + [(2 * k + 1, half * i) for i in range(3)]

    features = width * len(shifts)
    vmem = pl.BlockSpec(memory_space=pltpu.VMEM)
    smem, hbm = pl.BlockSpec(memory_space=pltpu.SMEM), pl.BlockSpec(memory_space=pl.ANY)
    normed = pltpu.VMEM((half, features), jnp.bfloat16)
    whole_weight = pltpu.VMEM((features, 3 * local), jnp.bfloat16)

    def first_kernel(*refs):
        first_half_kernel(first_slots, len(first_blocks), strip, *refs)

    def second_kernel(*refs):
        second_half_kernel(second_slots, len(second_blocks), strip, *refs)

    first_sums, all_gain = pl.pallas_call(
        first_kernel,
        out_shape=(
            jax.ShapeDtypeStruct((half, 3 * local), jnp.bfloat16),
            jax.ShapeDtypeStruct((1, features), jnp.float32),
        ),
        in_specs=[smem] + [vmem] * len(first_blocks) + [hbm],
        out_specs=(vmem, vmem),
        scratch_shapes=[normed, whole_weight, pltpu.SemaphoreType.DMA],
        name="norm_project",
    )(places, *first_blocks, weight)
    return pl.pallas_call(
        second_kernel,
        out_shape=jax.ShapeDtypeStruct((rows, local), jnp.bfloat16),
        in_specs=[smem] + [vmem] * len(second_blocks) + [hbm] + [vmem] * 4,
        out_specs=vmem,
        scratch_shapes=[
            normed,
            whole_weight,
            pltpu.VMEM((rows, 3 * local), jnp.bfloat16),
            pltpu.SemaphoreType.DMA,
        ],
        name="norm_project_attend",
    )(places, *second_blocks, weight, first_sums, all_gain, segment[:, None], segment[None, :])


def solution(mesh):
    return jax.shard_map(
        shards,
        mesh=mesh,
        in_specs=(
            P("dp", "tensor"),
            P("tensor"),
            P("dp", "tensor"),
            P("dp", "tensor"),
            P("dp", "tensor"),
            P(),
            P(),
        ),
        out_specs=P("dp", "tensor"),
        check_vma=False,
    )
```

```python
import math

import jax
import jax.numpy as jnp
from jax import lax
from jax.experimental import pallas as pl
from jax.experimental.pallas import tpu as pltpu
from jax.sharding import PartitionSpec as P

HEAD_DIM = 128
NORM_EPSILON = 1e-06
Z_PARTS, Y_PARTS = 4, 4
GAIN_ROWS = 16
ROW_TILE = 16


def z_shift(step):
    return [
        (z * Y_PARTS + y, (z + step) % Z_PARTS * Y_PARTS + y)
        for z in range(Z_PARTS)
        for y in range(Y_PARTS)
    ]


def y_shift(step):
    return [
        (z * Y_PARTS + y, z * Y_PARTS + (y + step) % Y_PARTS)
        for z in range(Z_PARTS)
        for y in range(Y_PARTS)
    ]


def dp_groups(varying):
    groups = {}
    for x in range(4):
        for z in range(4):
            for core in range(2):
                key = tuple(v for name, v in (("x", x), ("z", z), ("c", core)) if name not in varying)
                groups.setdefault(key, []).append(x * 8 + z * 2 + core)
    return list(groups.values())


def load_weights(source_ref, weight_ref, sem, strip):
    copies = []
    for x in range(4):
        for z in range(4):
            for core in range(2):
                held, wanted = (x * 2 + core) * 4 + z, x * 8 + z * 2 + core
                copies.append(
                    pltpu.make_async_copy(
                        source_ref.at[pl.ds(held * strip, strip), :],
                        weight_ref.at[pl.ds(wanted * strip, strip), :],
                        sem,
                    )
                )
    for copy in copies:
        copy.start()
    return copies


def slot_columns(places_ref, count, width):
    return [pl.ds(pl.multiple_of(places_ref[j] * width, 128), width) for j in range(count)]


def normalize(sources, gains, columns, first, last, normed_ref):
    features = normed_ref.shape[1]

    def step(i, carry):
        at = pl.multiple_of(first + i * ROW_TILE, ROW_TILE)

        def load(j):
            ref, shift = sources[j]
            return ref[pl.ds(at + shift, ROW_TILE), :].astype(jnp.float32)

        total = load(0)
        for j in range(1, len(sources)):
            total = total + load(j)
        mean = jnp.sum(total, axis=1, keepdims=True) * (1.0 / features)
        square = jnp.square(load(0) - mean)
        for j in range(1, len(sources)):
            square = square + jnp.square(load(j) - mean)
        var = jnp.sum(square, axis=1, keepdims=True) * (1.0 / features)
        scale = lax.rsqrt(var + NORM_EPSILON)
        for j in range(len(sources)):
            normed_ref[pl.ds(at, ROW_TILE), columns[j]] = (
                (load(j) - mean) * scale * gains[j]
            ).astype(jnp.bfloat16)
        return carry

    lax.fori_loop(0, (last - first) // ROW_TILE, step, 0)


def project_attend_kernel(slots, count, rows, cut, strip, *refs):
    places_ref, blocks = refs[0], refs[1 : 1 + count]
    source_ref, seg_col_ref, seg_row_ref, out_ref = refs[1 + count : 5 + count]
    normed_ref, weight_ref, sums_ref, sem = refs[5 + count :]
    copies = load_weights(source_ref, weight_ref, sem, strip)
    columns = slot_columns(places_ref, len(slots), blocks[0].shape[1])

    def part(pieces, row):
        for ref, start, first, last in pieces:
            if first <= row < last:
                return blocks[ref], start - first

    gains = []
    for pieces in slots:
        ref, shift = part(pieces, rows)
        gains.append(ref[pl.ds(rows + shift, GAIN_ROWS), :][:1].astype(jnp.float32))
    for first, last in ((0, cut), (cut, rows)):
        sources = [part(pieces, first) for pieces in slots]
        normalize(sources, gains, columns, first, last, normed_ref)
    for copy in copies:
        copy.wait()
    sums_ref[...] = jnp.dot(
        normed_ref[...], weight_ref[...], preferred_element_type=jnp.float32
    ).astype(jnp.bfloat16)
    local = out_ref.shape[1]
    span, window = 128, 256
    for row in range(0, rows, span):
        low = min(max(row - (window - span) // 2, 0), rows - window)
        same = seg_col_ref[row : row + span, :1] == seg_row_ref[:1, low : low + window]
        for col in range(0, local, HEAD_DIM):
            query = sums_ref[row : row + span, col : col + HEAD_DIM]
            key = sums_ref[low : low + window, local + col : local + col + HEAD_DIM]
            value = sums_ref[low : low + window, 2 * local + col : 2 * local + col + HEAD_DIM]
            scores = lax.dot_general(
                query, key, (((1,), (1,)), ((), ())), preferred_element_type=jnp.float32
            ) * (1.0 / math.sqrt(HEAD_DIM))
            scores = jnp.where(same, scores, -jnp.inf)
            expo = jnp.exp(scores - jnp.max(scores, axis=1, keepdims=True))
            probs = (expo / jnp.sum(expo, axis=1, keepdims=True)).astype(jnp.bfloat16)
            out_ref[row : row + span, col : col + HEAD_DIM] = jnp.dot(
                probs, value, preferred_element_type=jnp.float32
            ).astype(jnp.bfloat16)


def shards(page_patches, gain, q_weight, k_weight, v_weight, pack_lengths, line_order):
    groups = lax.axis_size("dp")
    page_index = lax.axis_index("dp")
    width = page_patches.shape[1]
    slot_rows = page_patches.shape[0] // groups
    rows = slot_rows * groups // 2
    local = q_weight.shape[1]
    strip = q_weight.shape[0]
    weight = jnp.concatenate([q_weight, k_weight, v_weight], axis=1)
    weight = lax.all_gather(weight, "dp", axis=0, tiled=True, axis_index_groups=dp_groups("z"))
    targets = jnp.arange(groups, dtype=jnp.int32)
    my_order = lax.dynamic_index_in_dim(line_order, page_index, 0, keepdims=False)
    slot_for = jnp.sum(
        jnp.where(my_order[None, :] == targets[:, None], targets[None, :], 0), axis=1
    )
    slots = page_patches.reshape(groups, slot_rows, width)
    outgoing = jnp.take(slots, slot_for, axis=0)
    incoming = lax.all_to_all(outgoing, "dp", split_axis=0, concat_axis=0, tiled=True)
    my_lengths = lax.dynamic_index_in_dim(pack_lengths, page_index, 0, keepdims=False)
    line_ends = jnp.cumsum(my_lengths)
    line_starts = line_ends - my_lengths
    row_ids = jnp.arange(rows, dtype=jnp.int32)
    segment = jnp.sum((line_ends[None, :] <= row_ids[:, None]).astype(jnp.int32), axis=1)
    start_of_row = jnp.sum(
        jnp.where(segment[:, None] == targets[None, :], line_starts[None, :], 0), axis=1
    )
    source_rows = segment * slot_rows + row_ids - start_of_row
    packed = jnp.take(incoming.reshape(groups * slot_rows, width), source_rows, axis=0)

    own = jnp.concatenate([packed, jnp.broadcast_to(gain[None, :], (GAIN_ROWS, width))], axis=0)
    all_rows = rows + GAIN_ROWS
    cut = rows // 2 + GAIN_ROWS

    def along_y(block, step):
        return lax.ppermute(block, "tensor", y_shift(step))

    def along_z(block, step):
        return lax.ppermute(block, "tensor", z_shift(step))

    own_far, own_down, own_up, z_down, z_up, weight = lax.optimization_barrier(
        (
            along_y(own, 2),
            along_y(own, -1),
            along_y(own, 1),
            along_z(own, -1),
            along_z(own, 1),
            weight,
        )
    )
    weight = lax.all_gather(weight, "dp", axis=0, tiled=True, axis_index_groups=dp_groups("xc"))
    pair = jnp.concatenate([z_up, z_down], axis=0)
    pair_down, pair_up, far_rest, far_top = lax.optimization_barrier(
        (along_y(pair, -1), along_y(pair, 1), along_z(z_down[cut:], -1), along_z(z_up[:cut], 1))
    )
    far = jnp.concatenate([far_top, far_rest], axis=0)
    far_far, far_down, far_up = along_y(far, 2), along_y(far, -1), along_y(far, 1)
    pair_far_up = along_y(pair_up[:all_rows], 1)
    pair_far_down = along_y(pair_down[all_rows:], -1)

    blocks, slots_at, shifts = [], [], []

    def add(array, dy, *dzs):
        blocks.append(array)
        for k, dz in enumerate(dzs):
            slots_at.append(((len(blocks) - 1, k * all_rows, 0, all_rows),))
            shifts.append((dz, dy))

    add(own, 0, 0)
    add(own_up, -1, 0)
    add(own_down, 1, 0)
    add(own_far, 2, 0)
    add(pair, 0, -1, 1)
    add(pair_up, -1, -1, 1)
    add(pair_down, 1, -1, 1)
    add(pair_far_up, 2, -1)
    add(pair_far_down, 2, 1)
    add(far, 0, 2)
    add(far_up, -1, 2)
    add(far_down, 1, 2)
    add(far_far, 2, 2)
    tensor = lax.axis_index("tensor")
    my_z, my_y = tensor // Y_PARTS, tensor % Y_PARTS
    step_z = jnp.array([dz for dz, _ in shifts], jnp.int32)
    step_y = jnp.array([dy for _, dy in shifts], jnp.int32)
    places = (my_z + step_z + Z_PARTS) % Z_PARTS * Y_PARTS + (my_y + step_y + Y_PARTS) % Y_PARTS

    def kernel(*refs):
        project_attend_kernel(slots_at, len(blocks), rows, cut, strip, *refs)

    features = width * len(slots_at)
    vmem = pl.BlockSpec(memory_space=pltpu.VMEM)
    smem, hbm = pl.BlockSpec(memory_space=pltpu.SMEM), pl.BlockSpec(memory_space=pl.ANY)
    return pl.pallas_call(
        kernel,
        out_shape=jax.ShapeDtypeStruct((rows, local), jnp.bfloat16),
        in_specs=[smem] + [vmem] * len(blocks) + [hbm, vmem, vmem],
        out_specs=vmem,
        scratch_shapes=[
            pltpu.VMEM((rows, features), jnp.bfloat16),
            pltpu.VMEM((features, 3 * local), jnp.bfloat16),
            pltpu.VMEM((rows, 3 * local), jnp.bfloat16),
            pltpu.SemaphoreType.DMA,
        ],
        name="norm_project_attend",
    )(places, *blocks, weight, segment[:, None], segment[None, :])


def solution(mesh):
    return jax.shard_map(
        shards,
        mesh=mesh,
        in_specs=(
            P("dp", "tensor"),
            P("tensor"),
            P("dp", "tensor"),
            P("dp", "tensor"),
            P("dp", "tensor"),
            P(),
            P(),
        ),
        out_specs=P("dp", "tensor"),
        check_vma=False,
    )
```

```python
import functools
import math

import jax
import jax.numpy as jnp
from jax import lax
from jax.experimental import pallas as pl
from jax.experimental.pallas import tpu as pltpu
from jax.sharding import PartitionSpec as P

HEAD_DIM = 128
NORM_EPSILON = 1e-06
Z_PARTS, Y_PARTS = 4, 4
GAIN_ROWS = 16
ROW_TILE = 16


def z_shift(step):
    return [
        (z * Y_PARTS + y, (z + step) % Z_PARTS * Y_PARTS + y)
        for z in range(Z_PARTS)
        for y in range(Y_PARTS)
    ]


def y_shift(step):
    return [
        (z * Y_PARTS + y, z * Y_PARTS + (y + step) % Y_PARTS)
        for z in range(Z_PARTS)
        for y in range(Y_PARTS)
    ]


def slot_columns(places_ref, count, width):
    return [pl.ds(pl.multiple_of(places_ref[j] * width, 128), width) for j in range(count)]


def moments(loads, width):
    count = width * len(loads)
    total = loads[0]()
    for load in loads[1:]:
        total = total + load()
    mean = jnp.sum(total, axis=1, keepdims=True) * (1.0 / count)
    square = jnp.square(loads[0]() - mean)
    for load in loads[1:]:
        square = square + jnp.square(load() - mean)
    return mean, jnp.sum(square, axis=1, keepdims=True)


def row_loads(blocks, slots, at):
    def load(ref, shift):
        return blocks[ref][pl.ds(at + shift, ROW_TILE), :].astype(jnp.float32)

    return [functools.partial(load, ref, shift) for ref, shift in slots]


def moments_kernel(slots, count, *refs):
    blocks, (mean_ref, square_ref) = refs[:count], refs[count:]
    width, lanes = blocks[0].shape[1], mean_ref.shape[1]

    def step(i, carry):
        at = pl.multiple_of(i * ROW_TILE, ROW_TILE)
        mean, square = moments(row_loads(blocks, slots, at), width)
        mean_ref[pl.ds(at, ROW_TILE), :] = jnp.broadcast_to(mean, (ROW_TILE, lanes))
        square_ref[pl.ds(at, ROW_TILE), :] = jnp.broadcast_to(square, (ROW_TILE, lanes))
        return carry

    lax.fori_loop(0, mean_ref.shape[0] // ROW_TILE, step, 0)


def project_attend_kernel(slots, known, count, rows, *refs):
    places_ref, blocks = refs[0], refs[1 : 1 + count]
    mean_ref, square_ref, source_ref, seg_col_ref, seg_row_ref, out_ref = refs[1 + count : 7 + count]
    normed_ref, weight_ref, sums_ref, sem = refs[7 + count :]
    copies = [pltpu.make_async_copy(source_ref, weight_ref, sem)]
    for copy in copies:
        copy.start()
    width, features = blocks[0].shape[1], normed_ref.shape[1]
    columns = slot_columns(places_ref, len(slots), width)
    gains = [
        blocks[ref][pl.ds(rows + shift, GAIN_ROWS), :][:1].astype(jnp.float32)
        for ref, shift in slots
    ]
    known_share = known * width / features
    last_share = 1.0 - known_share

    def step(i, carry):
        at = pl.multiple_of(i * ROW_TILE, ROW_TILE)
        loads = row_loads(blocks, slots, at)
        known_mean = mean_ref[pl.ds(at, ROW_TILE), :1]
        known_square = square_ref[pl.ds(at, ROW_TILE), :1]
        last_mean, last_square = moments(loads[known:], width)
        gap = last_mean - known_mean
        mean = known_mean + gap * last_share
        var = (known_square + last_square) * (1.0 / features) + jnp.square(gap) * (
            known_share * last_share
        )
        scale = lax.rsqrt(var + NORM_EPSILON)
        for j, load in enumerate(loads):
            normed_ref[pl.ds(at, ROW_TILE), columns[j]] = (
                (load() - mean) * scale * gains[j]
            ).astype(jnp.bfloat16)
        return carry

    lax.fori_loop(0, rows // ROW_TILE, step, 0)
    for copy in copies:
        copy.wait()
    sums_ref[...] = jnp.dot(
        normed_ref[...], weight_ref[...], preferred_element_type=jnp.float32
    ).astype(jnp.bfloat16)
    local = out_ref.shape[1]
    span, window = 128, 256
    for row in range(0, rows, span):
        low = min(max(row - (window - span) // 2, 0), rows - window)
        same = seg_col_ref[row : row + span, :1] == seg_row_ref[:1, low : low + window]
        for col in range(0, local, HEAD_DIM):
            query = sums_ref[row : row + span, col : col + HEAD_DIM]
            key = sums_ref[low : low + window, local + col : local + col + HEAD_DIM]
            value = sums_ref[low : low + window, 2 * local + col : 2 * local + col + HEAD_DIM]
            scores = lax.dot_general(
                query, key, (((1,), (1,)), ((), ())), preferred_element_type=jnp.float32
            ) * (1.0 / math.sqrt(HEAD_DIM))
            scores = jnp.where(same, scores, -jnp.inf)
            expo = jnp.exp(scores - jnp.max(scores, axis=1, keepdims=True))
            probs = (expo / jnp.sum(expo, axis=1, keepdims=True)).astype(jnp.bfloat16)
            out_ref[row : row + span, col : col + HEAD_DIM] = jnp.dot(
                probs, value, preferred_element_type=jnp.float32
            ).astype(jnp.bfloat16)


def shards(page_patches, gain, q_weight, k_weight, v_weight, pack_lengths, line_order):
    groups = lax.axis_size("dp")
    page_index = lax.axis_index("dp")
    width = page_patches.shape[1]
    slot_rows = page_patches.shape[0] // groups
    rows = slot_rows * groups // 2
    local = q_weight.shape[1]
    weight = jnp.concatenate([q_weight, k_weight, v_weight], axis=1)
    targets = jnp.arange(groups, dtype=jnp.int32)
    my_order = lax.dynamic_index_in_dim(line_order, page_index, 0, keepdims=False)
    slot_for = jnp.sum(
        jnp.where(my_order[None, :] == targets[:, None], targets[None, :], 0), axis=1
    )
    slots = page_patches.reshape(groups, slot_rows, width)
    outgoing = jnp.take(slots, slot_for, axis=0)
    outgoing, weight = lax.optimization_barrier((outgoing, weight))
    weight = lax.all_gather(weight, "dp", axis=0, tiled=True)
    incoming = lax.all_to_all(outgoing, "dp", split_axis=0, concat_axis=0, tiled=True)
    my_lengths = lax.dynamic_index_in_dim(pack_lengths, page_index, 0, keepdims=False)
    line_ends = jnp.cumsum(my_lengths)
    line_starts = line_ends - my_lengths
    row_ids = jnp.arange(rows, dtype=jnp.int32)
    segment = jnp.sum((line_ends[None, :] <= row_ids[:, None]).astype(jnp.int32), axis=1)
    start_of_row = jnp.sum(
        jnp.where(segment[:, None] == targets[None, :], line_starts[None, :], 0), axis=1
    )
    source_rows = segment * slot_rows + row_ids - start_of_row
    packed = jnp.take(incoming.reshape(groups * slot_rows, width), source_rows, axis=0)

    own = jnp.concatenate([packed, jnp.broadcast_to(gain[None, :], (GAIN_ROWS, width))], axis=0)
    all_rows = rows + GAIN_ROWS
    cut = rows // 2 + GAIN_ROWS

    def along_y(block, step):
        return lax.ppermute(block, "tensor", y_shift(step))

    def along_z(block, step):
        return lax.ppermute(block, "tensor", z_shift(step))

    own_far, own_down, own_up, z_down, z_up = lax.optimization_barrier(
        (
            along_y(own, 2),
            along_y(own, -1),
            along_y(own, 1),
            along_z(own, -1),
            along_z(own, 1),
        )
    )
    pair = jnp.concatenate([z_up, z_down], axis=0)
    pair_up, pair_down = along_y(pair, 1), along_y(pair, -1)
    pair_far_up = along_y(pair_up[:all_rows], 1)
    pair_far_down = along_y(pair_down[all_rows:], -1)
    far_top, far_rest = along_z(z_up[:cut], 1), along_z(z_down[cut:], -1)
    far = jnp.concatenate([far_top, far_rest], axis=0)
    far_far, far_down, far_up = along_y(far, 2), along_y(far, -1), along_y(far, 1)

    blocks, slots_at, shifts = [], [], []

    def add(array, dy, *dzs):
        blocks.append(array)
        for k, dz in enumerate(dzs):
            slots_at.append((len(blocks) - 1, k * all_rows))
            shifts.append((dz, dy))

    add(own, 0, 0)
    add(own_up, -1, 0)
    add(own_down, 1, 0)
    add(own_far, 2, 0)
    add(pair, 0, -1, 1)
    add(pair_up, -1, -1, 1)
    add(pair_down, 1, -1, 1)
    add(pair_far_up, 2, -1)
    add(pair_far_down, 2, 1)
    known, known_blocks = len(slots_at), list(blocks)
    add(far, 0, 2)
    add(far_up, -1, 2)
    add(far_down, 1, 2)
    add(far_far, 2, 2)
    tensor = lax.axis_index("tensor")
    my_z, my_y = tensor // Y_PARTS, tensor % Y_PARTS
    step_z = jnp.array([dz for dz, _ in shifts], jnp.int32)
    step_y = jnp.array([dy for _, dy in shifts], jnp.int32)
    places = (my_z + step_z + Z_PARTS) % Z_PARTS * Y_PARTS + (my_y + step_y + Y_PARTS) % Y_PARTS

    def first_kernel(*refs):
        moments_kernel(slots_at[:known], len(known_blocks), *refs)

    def last_kernel(*refs):
        project_attend_kernel(slots_at, known, len(blocks), rows, *refs)

    features = width * len(slots_at)
    vmem = pl.BlockSpec(memory_space=pltpu.VMEM)
    smem, hbm = pl.BlockSpec(memory_space=pltpu.SMEM), pl.BlockSpec(memory_space=pl.ANY)
    row_figure = jax.ShapeDtypeStruct((rows, 128), jnp.float32)
    known_mean, known_square = pl.pallas_call(
        first_kernel,
        out_shape=(row_figure, row_figure),
        in_specs=[vmem] * len(known_blocks),
        out_specs=(vmem, vmem),
        name="row_moments",
    )(*known_blocks)
    return pl.pallas_call(
        last_kernel,
        out_shape=jax.ShapeDtypeStruct((rows, local), jnp.bfloat16),
        in_specs=[smem] + [vmem] * (len(blocks) + 2) + [hbm, vmem, vmem],
        out_specs=vmem,
        scratch_shapes=[
            pltpu.VMEM((rows, features), jnp.bfloat16),
            pltpu.VMEM((features, 3 * local), jnp.bfloat16),
            pltpu.VMEM((rows, 3 * local), jnp.bfloat16),
            pltpu.SemaphoreType.DMA,
        ],
        name="norm_project_attend",
    )(
        places,
        *blocks,
        known_mean,
        known_square,
        weight,
        segment[:, None],
        segment[None, :],
    )


def solution(mesh):
    return jax.shard_map(
        shards,
        mesh=mesh,
        in_specs=(
            P("dp", "tensor"),
            P("tensor"),
            P("dp", "tensor"),
            P("dp", "tensor"),
            P("dp", "tensor"),
            P(),
            P(),
        ),
        out_specs=P("dp", "tensor"),
        check_vma=False,
    )
```

```python
import functools
import math

import jax
import jax.numpy as jnp
from jax import lax
from jax.experimental import pallas as pl
from jax.experimental.pallas import tpu as pltpu
from jax.sharding import PartitionSpec as P

HEAD_DIM = 128
NORM_EPSILON = 1e-06
Z_PARTS, Y_PARTS = 4, 4
GAIN_ROWS = 16
ROW_TILE = 16


def z_shift(step):
    return [
        (z * Y_PARTS + y, (z + step) % Z_PARTS * Y_PARTS + y)
        for z in range(Z_PARTS)
        for y in range(Y_PARTS)
    ]


def y_shift(step):
    return [
        (z * Y_PARTS + y, z * Y_PARTS + (y + step) % Y_PARTS)
        for z in range(Z_PARTS)
        for y in range(Y_PARTS)
    ]


def dp_groups(varying):
    groups = {}
    for x in range(4):
        for z in range(4):
            for core in range(2):
                key = tuple(v for name, v in (("x", x), ("z", z), ("c", core)) if name not in varying)
                groups.setdefault(key, []).append(x * 8 + z * 2 + core)
    return list(groups.values())


def load_weights(source_ref, weight_ref, sem, strip):
    copies = []
    for x in range(4):
        for z in range(4):
            for core in range(2):
                held, wanted = (x * 2 + core) * 4 + z, x * 8 + z * 2 + core
                copies.append(
                    pltpu.make_async_copy(
                        source_ref.at[pl.ds(held * strip, strip), :],
                        weight_ref.at[pl.ds(wanted * strip, strip), :],
                        sem,
                    )
                )
    for copy in copies:
        copy.start()
    return copies


def slot_columns(places_ref, count, width):
    return [pl.ds(pl.multiple_of(places_ref[j] * width, 128), width) for j in range(count)]


def moments(loads, width):
    count = width * len(loads)
    total = loads[0]()
    for load in loads[1:]:
        total = total + load()
    mean = jnp.sum(total, axis=1, keepdims=True) * (1.0 / count)
    square = jnp.square(loads[0]() - mean)
    for load in loads[1:]:
        square = square + jnp.square(load() - mean)
    return mean, jnp.sum(square, axis=1, keepdims=True)


def row_loads(blocks, slots, at):
    def load(ref, shift):
        return blocks[ref][pl.ds(at + shift, ROW_TILE), :].astype(jnp.float32)

    return [functools.partial(load, ref, shift) for ref, shift in slots]


def moments_kernel(slots, count, *refs):
    blocks, (mean_ref, square_ref) = refs[:count], refs[count:]
    width, lanes = blocks[0].shape[1], mean_ref.shape[1]

    def step(i, carry):
        at = pl.multiple_of(i * ROW_TILE, ROW_TILE)
        mean, square = moments(row_loads(blocks, slots, at), width)
        mean_ref[pl.ds(at, ROW_TILE), :] = jnp.broadcast_to(mean, (ROW_TILE, lanes))
        square_ref[pl.ds(at, ROW_TILE), :] = jnp.broadcast_to(square, (ROW_TILE, lanes))
        return carry

    lax.fori_loop(0, mean_ref.shape[0] // ROW_TILE, step, 0)


def project_attend_kernel(slots, known, count, rows, strip, *refs):
    places_ref, blocks = refs[0], refs[1 : 1 + count]
    mean_ref, square_ref, source_ref, seg_col_ref, seg_row_ref, out_ref = refs[1 + count : 7 + count]
    normed_ref, weight_ref, sums_ref, sem = refs[7 + count :]
    copies = load_weights(source_ref, weight_ref, sem, strip)
    width, features = blocks[0].shape[1], normed_ref.shape[1]
    columns = slot_columns(places_ref, len(slots), width)
    gains = [
        blocks[ref][pl.ds(rows + shift, GAIN_ROWS), :][:1].astype(jnp.float32)
        for ref, shift in slots
    ]
    known_share = known * width / features
    last_share = 1.0 - known_share

    def step(i, carry):
        at = pl.multiple_of(i * ROW_TILE, ROW_TILE)
        loads = row_loads(blocks, slots, at)
        known_mean = mean_ref[pl.ds(at, ROW_TILE), :1]
        known_square = square_ref[pl.ds(at, ROW_TILE), :1]
        last_mean, last_square = moments(loads[known:], width)
        gap = last_mean - known_mean
        mean = known_mean + gap * last_share
        var = (known_square + last_square) * (1.0 / features) + jnp.square(gap) * (
            known_share * last_share
        )
        scale = lax.rsqrt(var + NORM_EPSILON)
        for j, load in enumerate(loads):
            normed_ref[pl.ds(at, ROW_TILE), columns[j]] = (
                (load() - mean) * scale * gains[j]
            ).astype(jnp.bfloat16)
        return carry

    lax.fori_loop(0, rows // ROW_TILE, step, 0)
    for copy in copies:
        copy.wait()
    sums_ref[...] = jnp.dot(
        normed_ref[...], weight_ref[...], preferred_element_type=jnp.float32
    ).astype(jnp.bfloat16)
    local = out_ref.shape[1]
    span, window = 128, 256
    for row in range(0, rows, span):
        low = min(max(row - (window - span) // 2, 0), rows - window)
        same = seg_col_ref[row : row + span, :1] == seg_row_ref[:1, low : low + window]
        for col in range(0, local, HEAD_DIM):
            query = sums_ref[row : row + span, col : col + HEAD_DIM]
            key = sums_ref[low : low + window, local + col : local + col + HEAD_DIM]
            value = sums_ref[low : low + window, 2 * local + col : 2 * local + col + HEAD_DIM]
            scores = lax.dot_general(
                query, key, (((1,), (1,)), ((), ())), preferred_element_type=jnp.float32
            ) * (1.0 / math.sqrt(HEAD_DIM))
            scores = jnp.where(same, scores, -jnp.inf)
            expo = jnp.exp(scores - jnp.max(scores, axis=1, keepdims=True))
            probs = (expo / jnp.sum(expo, axis=1, keepdims=True)).astype(jnp.bfloat16)
            out_ref[row : row + span, col : col + HEAD_DIM] = jnp.dot(
                probs, value, preferred_element_type=jnp.float32
            ).astype(jnp.bfloat16)


def shards(page_patches, gain, q_weight, k_weight, v_weight, pack_lengths, line_order):
    groups = lax.axis_size("dp")
    page_index = lax.axis_index("dp")
    width = page_patches.shape[1]
    slot_rows = page_patches.shape[0] // groups
    rows = slot_rows * groups // 2
    local = q_weight.shape[1]
    weight = jnp.concatenate([q_weight, k_weight, v_weight], axis=1)
    targets = jnp.arange(groups, dtype=jnp.int32)
    my_order = lax.dynamic_index_in_dim(line_order, page_index, 0, keepdims=False)
    slot_for = jnp.sum(
        jnp.where(my_order[None, :] == targets[:, None], targets[None, :], 0), axis=1
    )
    slots = page_patches.reshape(groups, slot_rows, width)
    outgoing = jnp.take(slots, slot_for, axis=0)
    outgoing, weight = lax.optimization_barrier((outgoing, weight))
    weight = lax.all_gather(weight, "dp", axis=0, tiled=True, axis_index_groups=dp_groups("z"))
    incoming = lax.all_to_all(outgoing, "dp", split_axis=0, concat_axis=0, tiled=True)
    my_lengths = lax.dynamic_index_in_dim(pack_lengths, page_index, 0, keepdims=False)
    line_ends = jnp.cumsum(my_lengths)
    line_starts = line_ends - my_lengths
    row_ids = jnp.arange(rows, dtype=jnp.int32)
    segment = jnp.sum((line_ends[None, :] <= row_ids[:, None]).astype(jnp.int32), axis=1)
    start_of_row = jnp.sum(
        jnp.where(segment[:, None] == targets[None, :], line_starts[None, :], 0), axis=1
    )
    source_rows = segment * slot_rows + row_ids - start_of_row
    packed = jnp.take(incoming.reshape(groups * slot_rows, width), source_rows, axis=0)

    own = jnp.concatenate([packed, jnp.broadcast_to(gain[None, :], (GAIN_ROWS, width))], axis=0)
    all_rows = rows + GAIN_ROWS
    cut = rows // 2 + GAIN_ROWS

    def along_y(block, step):
        return lax.ppermute(block, "tensor", y_shift(step))

    def along_z(block, step):
        return lax.ppermute(block, "tensor", z_shift(step))

    own_far, own_down, own_up, z_down, z_up, weight = lax.optimization_barrier(
        (
            along_y(own, 2),
            along_y(own, -1),
            along_y(own, 1),
            along_z(own, -1),
            along_z(own, 1),
            weight,
        )
    )
    weight = lax.all_gather(weight, "dp", axis=0, tiled=True, axis_index_groups=dp_groups("xc"))
    pair = jnp.concatenate([z_up, z_down], axis=0)
    pair_up, pair_down = along_y(pair, 1), along_y(pair, -1)
    pair_far_up = along_y(pair_up[:all_rows], 1)
    pair_far_down = along_y(pair_down[all_rows:], -1)
    far_top, far_rest = along_z(z_up[:cut], 1), along_z(z_down[cut:], -1)
    far_top, far_rest, pair_up, pair_down = lax.optimization_barrier(
        (far_top, far_rest, pair_up, pair_down)
    )
    far = jnp.concatenate([far_top, far_rest], axis=0)
    far_far, far_down, far_up = along_y(far, 2), along_y(far, -1), along_y(far, 1)

    blocks, slots_at, shifts = [], [], []

    def add(array, dy, *dzs):
        blocks.append(array)
        for k, dz in enumerate(dzs):
            slots_at.append((len(blocks) - 1, k * all_rows))
            shifts.append((dz, dy))

    add(own, 0, 0)
    add(own_up, -1, 0)
    add(own_down, 1, 0)
    add(own_far, 2, 0)
    add(pair, 0, -1, 1)
    add(pair_up, -1, -1, 1)
    add(pair_down, 1, -1, 1)
    known, known_blocks = len(slots_at), list(blocks)
    add(pair_far_up, 2, -1)
    add(pair_far_down, 2, 1)
    add(far, 0, 2)
    add(far_up, -1, 2)
    add(far_down, 1, 2)
    add(far_far, 2, 2)
    tensor = lax.axis_index("tensor")
    my_z, my_y = tensor // Y_PARTS, tensor % Y_PARTS
    step_z = jnp.array([dz for dz, _ in shifts], jnp.int32)
    step_y = jnp.array([dy for _, dy in shifts], jnp.int32)
    places = (my_z + step_z + Z_PARTS) % Z_PARTS * Y_PARTS + (my_y + step_y + Y_PARTS) % Y_PARTS

    def first_kernel(*refs):
        moments_kernel(slots_at[:known], len(known_blocks), *refs)

    def last_kernel(*refs):
        project_attend_kernel(slots_at, known, len(blocks), rows, q_weight.shape[0], *refs)

    features = width * len(slots_at)
    vmem = pl.BlockSpec(memory_space=pltpu.VMEM)
    smem, hbm = pl.BlockSpec(memory_space=pltpu.SMEM), pl.BlockSpec(memory_space=pl.ANY)
    row_figure = jax.ShapeDtypeStruct((rows, 128), jnp.float32)
    known_mean, known_square = pl.pallas_call(
        first_kernel,
        out_shape=(row_figure, row_figure),
        in_specs=[vmem] * len(known_blocks),
        out_specs=(vmem, vmem),
        name="row_moments",
    )(*known_blocks)
    return pl.pallas_call(
        last_kernel,
        out_shape=jax.ShapeDtypeStruct((rows, local), jnp.bfloat16),
        in_specs=[smem] + [vmem] * (len(blocks) + 2) + [hbm, vmem, vmem],
        out_specs=vmem,
        scratch_shapes=[
            pltpu.VMEM((rows, features), jnp.bfloat16),
            pltpu.VMEM((features, 3 * local), jnp.bfloat16),
            pltpu.VMEM((rows, 3 * local), jnp.bfloat16),
            pltpu.SemaphoreType.DMA,
        ],
        name="norm_project_attend",
    )(
        places,
        *blocks,
        known_mean,
        known_square,
        weight,
        segment[:, None],
        segment[None, :],
    )


def solution(mesh):
    return jax.shard_map(
        shards,
        mesh=mesh,
        in_specs=(
            P("dp", "tensor"),
            P("tensor"),
            P("dp", "tensor"),
            P("dp", "tensor"),
            P("dp", "tensor"),
            P(),
            P(),
        ),
        out_specs=P("dp", "tensor"),
        check_vma=False,
    )
```

```python
import math

import jax
import jax.numpy as jnp
from jax import lax
from jax.experimental import pallas as pl
from jax.experimental.pallas import tpu as pltpu
from jax.sharding import PartitionSpec as P

HEAD_DIM = 128
NORM_EPSILON = 1e-06
Z_PARTS, Y_PARTS = 4, 4
GAIN_ROWS = 16
ROW_TILE = 16


def z_shift(step):
    return [
        (z * Y_PARTS + y, (z + step) % Z_PARTS * Y_PARTS + y)
        for z in range(Z_PARTS)
        for y in range(Y_PARTS)
    ]


def y_shift(step):
    return [
        (z * Y_PARTS + y, z * Y_PARTS + (y + step) % Y_PARTS)
        for z in range(Z_PARTS)
        for y in range(Y_PARTS)
    ]


def dp_move(x_step, z_step, core_step):
    pairs = []
    for x in range(4):
        for z in range(4):
            for core in range(2):
                to = (x + x_step) % 4 * 8 + (z + z_step) % 4 * 2 + (core + core_step) % 2
                pairs.append((x * 8 + z * 2 + core, to))
    return pairs


def dp_groups(varying):
    groups = {}
    for x in range(4):
        for z in range(4):
            for core in range(2):
                key = tuple(v for name, v in (("x", x), ("z", z), ("c", core)) if name not in varying)
                groups.setdefault(key, []).append(x * 8 + z * 2 + core)
    return list(groups.values())


def load_weights(source_ref, weight_ref, sem, strip, my_lo):
    copies = []
    for x in range(4):
        for z in range(4):
            for core in range(2):
                held = (x * 2 + core) * 4 + z
                wanted = x * 8 + (my_lo - z + 4) % 4 * 2 + core
                at = pl.multiple_of(wanted * strip, strip)
                copies.append(
                    pltpu.make_async_copy(
                        source_ref.at[pl.ds(held * strip, strip), :],
                        weight_ref.at[pl.ds(at, strip), :],
                        sem,
                    )
                )
    for copy in copies:
        copy.start()
    return copies


def slot_columns(places_ref, count, width):
    return [pl.ds(pl.multiple_of(places_ref[j] * width, 128), width) for j in range(count)]


def normalize(sources, gains, columns, first, last, normed_ref):
    features = normed_ref.shape[1]

    def step(i, carry):
        at = pl.multiple_of(first + i * ROW_TILE, ROW_TILE)

        def load(j):
            ref, shift = sources[j]
            return ref[pl.ds(at + shift, ROW_TILE), :].astype(jnp.float32)

        total = load(0)
        for j in range(1, len(sources)):
            total = total + load(j)
        mean = jnp.sum(total, axis=1, keepdims=True) * (1.0 / features)
        square = jnp.square(load(0) - mean)
        for j in range(1, len(sources)):
            square = square + jnp.square(load(j) - mean)
        var = jnp.sum(square, axis=1, keepdims=True) * (1.0 / features)
        scale = lax.rsqrt(var + NORM_EPSILON)
        for j in range(len(sources)):
            normed_ref[pl.ds(at, ROW_TILE), columns[j]] = (
                (load(j) - mean) * scale * gains[j]
            ).astype(jnp.bfloat16)
        return carry

    lax.fori_loop(0, (last - first) // ROW_TILE, step, 0)


def project_attend_kernel(slots, count, rows, cut, strip, *refs):
    places_ref, blocks = refs[0], refs[1 : 1 + count]
    source_ref, seg_col_ref, seg_row_ref, out_ref = refs[1 + count : 5 + count]
    normed_ref, weight_ref, sums_ref, sem = refs[5 + count :]
    copies = load_weights(source_ref, weight_ref, sem, strip, places_ref[len(slots)])
    columns = slot_columns(places_ref, len(slots), blocks[0].shape[1])

    def part(pieces, row):
        for ref, start, first, last in pieces:
            if first <= row < last:
                return blocks[ref], start - first

    gains = []
    for pieces in slots:
        ref, shift = part(pieces, rows)
        gains.append(ref[pl.ds(rows + shift, GAIN_ROWS), :][:1].astype(jnp.float32))
    for first, last in ((0, cut), (cut, rows)):
        sources = [part(pieces, first) for pieces in slots]
        normalize(sources, gains, columns, first, last, normed_ref)
    for copy in copies:
        copy.wait()
    sums_ref[...] = jnp.dot(
        normed_ref[...], weight_ref[...], preferred_element_type=jnp.float32
    ).astype(jnp.bfloat16)
    local = out_ref.shape[1]
    span, window = 128, 256
    for row in range(0, rows, span):
        low = min(max(row - (window - span) // 2, 0), rows - window)
        same = seg_col_ref[row : row + span, :1] == seg_row_ref[:1, low : low + window]
        for col in range(0, local, HEAD_DIM):
            query = sums_ref[row : row + span, col : col + HEAD_DIM]
            key = sums_ref[low : low + window, local + col : local + col + HEAD_DIM]
            value = sums_ref[low : low + window, 2 * local + col : 2 * local + col + HEAD_DIM]
            scores = lax.dot_general(
                query, key, (((1,), (1,)), ((), ())), preferred_element_type=jnp.float32
            ) * (1.0 / math.sqrt(HEAD_DIM))
            scores = jnp.where(same, scores, -jnp.inf)
            expo = jnp.exp(scores - jnp.max(scores, axis=1, keepdims=True))
            probs = (expo / jnp.sum(expo, axis=1, keepdims=True)).astype(jnp.bfloat16)
            out_ref[row : row + span, col : col + HEAD_DIM] = jnp.dot(
                probs, value, preferred_element_type=jnp.float32
            ).astype(jnp.bfloat16)


def shards(page_patches, gain, q_weight, k_weight, v_weight, pack_lengths, line_order):
    groups = lax.axis_size("dp")
    page_index = lax.axis_index("dp")
    width = page_patches.shape[1]
    slot_rows = page_patches.shape[0] // groups
    rows = slot_rows * groups // 2
    local = q_weight.shape[1]
    strip = q_weight.shape[0]
    weight = jnp.concatenate([q_weight, k_weight, v_weight], axis=1)
    column = [lax.ppermute(weight, "dp", dp_move(0, k, 0)) for k in (1, 2, 3)]
    targets = jnp.arange(groups, dtype=jnp.int32)
    my_order = lax.dynamic_index_in_dim(line_order, page_index, 0, keepdims=False)
    slot_for = jnp.sum(
        jnp.where(my_order[None, :] == targets[:, None], targets[None, :], 0), axis=1
    )
    slots = page_patches.reshape(groups, slot_rows, width)
    outgoing = jnp.take(slots, slot_for, axis=0)
    incoming = lax.all_to_all(outgoing, "dp", split_axis=0, concat_axis=0, tiled=True)
    incoming, *column = lax.optimization_barrier((incoming, *column))
    weight = jnp.concatenate([weight] + column, axis=0)
    weight = lax.all_gather(weight, "dp", axis=0, tiled=True, axis_index_groups=dp_groups("xc"))
    my_lengths = lax.dynamic_index_in_dim(pack_lengths, page_index, 0, keepdims=False)
    line_ends = jnp.cumsum(my_lengths)
    line_starts = line_ends - my_lengths
    row_ids = jnp.arange(rows, dtype=jnp.int32)
    segment = jnp.sum((line_ends[None, :] <= row_ids[:, None]).astype(jnp.int32), axis=1)
    start_of_row = jnp.sum(
        jnp.where(segment[:, None] == targets[None, :], line_starts[None, :], 0), axis=1
    )
    source_rows = segment * slot_rows + row_ids - start_of_row
    packed = jnp.take(incoming.reshape(groups * slot_rows, width), source_rows, axis=0)

    own = jnp.concatenate([packed, jnp.broadcast_to(gain[None, :], (GAIN_ROWS, width))], axis=0)
    all_rows = rows + GAIN_ROWS
    cut = rows // 2 + GAIN_ROWS

    def along_y(block, step):
        return lax.ppermute(block, "tensor", y_shift(step))

    def along_z(block, step):
        return lax.ppermute(block, "tensor", z_shift(step))

    z_up, z_down, own_up, own_down, own_far = lax.optimization_barrier(
        (
            along_z(own, 1),
            along_z(own, -1),
            along_y(own, 1),
            along_y(own, -1),
            along_y(own, 2),
        )
    )
    pair = jnp.concatenate([z_up, z_down], axis=0)
    pair_up, pair_down = along_y(pair, 1), along_y(pair, -1)
    pair_far_up = along_y(pair_up[:all_rows], 1)
    pair_far_down = along_y(pair_down[all_rows:], -1)
    far_top, far_rest = along_z(z_up[:cut], 1), along_z(z_down[cut:], -1)
    far_top, far_rest, pair_up, pair_down = lax.optimization_barrier(
        (far_top, far_rest, pair_up, pair_down)
    )
    far = jnp.concatenate([far_top, far_rest], axis=0)
    far_far, far_down, far_up = along_y(far, 2), along_y(far, -1), along_y(far, 1)

    blocks, slots_at, shifts = [], [], []

    def add(array, dy, *dzs):
        blocks.append(array)
        for k, dz in enumerate(dzs):
            slots_at.append(((len(blocks) - 1, k * all_rows, 0, all_rows),))
            shifts.append((dz, dy))

    add(own, 0, 0)
    add(own_up, -1, 0)
    add(own_down, 1, 0)
    add(own_far, 2, 0)
    add(pair, 0, -1, 1)
    add(pair_up, -1, -1, 1)
    add(pair_down, 1, -1, 1)
    add(pair_far_up, 2, -1)
    add(pair_far_down, 2, 1)
    add(far, 0, 2)
    add(far_up, -1, 2)
    add(far_down, 1, 2)
    add(far_far, 2, 2)
    tensor = lax.axis_index("tensor")
    my_z, my_y = tensor // Y_PARTS, tensor % Y_PARTS
    step_z = jnp.array([dz for dz, _ in shifts], jnp.int32)
    step_y = jnp.array([dy for _, dy in shifts], jnp.int32)
    places = (my_z + step_z + Z_PARTS) % Z_PARTS * Y_PARTS + (my_y + step_y + Y_PARTS) % Y_PARTS

    places = jnp.concatenate([places, page_index[None] // 2 % 4])

    def kernel(*refs):
        project_attend_kernel(slots_at, len(blocks), rows, cut, strip, *refs)

    features = width * len(slots_at)
    vmem = pl.BlockSpec(memory_space=pltpu.VMEM)
    smem, hbm = pl.BlockSpec(memory_space=pltpu.SMEM), pl.BlockSpec(memory_space=pl.ANY)
    return pl.pallas_call(
        kernel,
        out_shape=jax.ShapeDtypeStruct((rows, local), jnp.bfloat16),
        in_specs=[smem] + [vmem] * len(blocks) + [hbm, vmem, vmem],
        out_specs=vmem,
        scratch_shapes=[
            pltpu.VMEM((rows, features), jnp.bfloat16),
            pltpu.VMEM((features, 3 * local), jnp.bfloat16),
            pltpu.VMEM((rows, 3 * local), jnp.bfloat16),
            pltpu.SemaphoreType.DMA,
        ],
        name="norm_project_attend",
    )(places, *blocks, weight, segment[:, None], segment[None, :])


def solution(mesh):
    return jax.shard_map(
        shards,
        mesh=mesh,
        in_specs=(
            P("dp", "tensor"),
            P("tensor"),
            P("dp", "tensor"),
            P("dp", "tensor"),
            P("dp", "tensor"),
            P(),
            P(),
        ),
        out_specs=P("dp", "tensor"),
        check_vma=False,
    )
```

```python
import math

import jax
import jax.numpy as jnp
from jax import lax
from jax.experimental import pallas as pl
from jax.experimental.pallas import tpu as pltpu
from jax.sharding import PartitionSpec as P

HEAD_DIM = 128
NORM_EPSILON = 1e-06
Z_PARTS, Y_PARTS = 4, 4
GAIN_ROWS = 16
ROW_TILE = 16


def z_shift(step):
    return [
        (z * Y_PARTS + y, (z + step) % Z_PARTS * Y_PARTS + y)
        for z in range(Z_PARTS)
        for y in range(Y_PARTS)
    ]


def y_shift(step):
    return [
        (z * Y_PARTS + y, z * Y_PARTS + (y + step) % Y_PARTS)
        for z in range(Z_PARTS)
        for y in range(Y_PARTS)
    ]


def dp_groups(varying):
    groups = {}
    for x in range(4):
        for z in range(4):
            for core in range(2):
                key = tuple(v for name, v in (("x", x), ("z", z), ("c", core)) if name not in varying)
                groups.setdefault(key, []).append(x * 8 + z * 2 + core)
    return list(groups.values())


def load_weights(source_ref, weight_ref, sem, strip):
    copies = []
    for x in range(4):
        for z in range(4):
            for core in range(2):
                held, wanted = (x * 2 + core) * 4 + z, x * 8 + z * 2 + core
                copies.append(
                    pltpu.make_async_copy(
                        source_ref.at[pl.ds(held * strip, strip), :],
                        weight_ref.at[pl.ds(wanted * strip, strip), :],
                        sem,
                    )
                )
    for copy in copies:
        copy.start()
    return copies


def slot_columns(places_ref, count, width):
    return [pl.ds(pl.multiple_of(places_ref[j] * width, 128), width) for j in range(count)]


def normalize(block_ref, gains, columns, row, normed_ref):
    features = normed_ref.shape[1]
    at = pl.multiple_of(row, ROW_TILE)

    def load(j):
        return block_ref[j, pl.ds(at, ROW_TILE), :].astype(jnp.float32)

    total = load(0)
    for j in range(1, len(gains)):
        total = total + load(j)
    mean = jnp.sum(total, axis=1, keepdims=True) * (1.0 / features)
    square = jnp.square(load(0) - mean)
    for j in range(1, len(gains)):
        square = square + jnp.square(load(j) - mean)
    var = jnp.sum(square, axis=1, keepdims=True) * (1.0 / features)
    scale = lax.rsqrt(var + NORM_EPSILON)
    for j in range(len(gains)):
        normed_ref[pl.ds(at, ROW_TILE), columns[j]] = (
            (load(j) - mean) * scale * gains[j]
        ).astype(jnp.bfloat16)


def project_attend_kernel(slots, count, rows, strip, *refs):
    places_ref, blocks = refs[0], refs[1 : 1 + count]
    source_ref, seg_col_ref, seg_row_ref, out_ref = refs[1 + count : 5 + count]
    block_ref, normed_ref, weight_ref, total_ref, sums_ref, sem, block_sem = refs[5 + count :]
    width, features = block_ref.shape[2], normed_ref.shape[1]
    half = rows // 2
    parts = [(rows, GAIN_ROWS)] + [(row, rows // 4) for row in range(0, rows, rows // 4)]
    block_copies = []
    for k, (row, size) in enumerate(parts):
        block_copies.append(
            [
                pltpu.make_async_copy(
                    blocks[ref].at[pl.ds(start + row, size), :],
                    block_ref.at[j, pl.ds(row, size), :],
                    block_sem.at[k],
                )
                for j, (ref, start) in enumerate(slots)
            ]
        )
    for copies in block_copies:
        for copy in copies:
            copy.start()
    weight_copies = load_weights(source_ref, weight_ref, sem, strip)
    columns = slot_columns(places_ref, len(slots), width)
    for copy in block_copies[0]:
        copy.wait()
    gains = [
        block_ref[j, pl.ds(rows, GAIN_ROWS), :][:1].astype(jnp.float32) for j in range(len(slots))
    ]

    for k in range(2):
        for copy in block_copies[1 + k]:
            copy.wait()

        def first_step(i, carry):
            normalize(block_ref, gains, columns, k * rows // 4 + i * ROW_TILE, normed_ref)
            return carry

        lax.fori_loop(0, rows // 4 // ROW_TILE, first_step, 0)

    for copies in (block_copies[3], block_copies[4], weight_copies):
        for copy in copies:
            copy.wait()
    steps = half // (2 * ROW_TILE)
    depth = features // steps
    total_ref[...] = jnp.zeros_like(total_ref)

    def second_step(i, carry):
        at = pl.ds(pl.multiple_of(i * depth, depth), depth)
        total_ref[...] += jnp.dot(
            normed_ref[:half, at], weight_ref[at, :], preferred_element_type=jnp.float32
        )
        for k in range(2):
            normalize(block_ref, gains, columns, half + (2 * i + k) * ROW_TILE, normed_ref)
        return carry

    lax.fori_loop(0, steps, second_step, 0)
    sums_ref[:half] = total_ref[...].astype(jnp.bfloat16)
    sums_ref[half:] = jnp.dot(
        normed_ref[half:], weight_ref[...], preferred_element_type=jnp.float32
    ).astype(jnp.bfloat16)
    local = out_ref.shape[1]
    span, window = 128, 256
    for row in range(0, rows, span):
        low = min(max(row - (window - span) // 2, 0), rows - window)
        same = seg_col_ref[row : row + span, :1] == seg_row_ref[:1, low : low + window]
        for col in range(0, local, HEAD_DIM):
            query = sums_ref[row : row + span, col : col + HEAD_DIM]
            key = sums_ref[low : low + window, local + col : local + col + HEAD_DIM]
            value = sums_ref[low : low + window, 2 * local + col : 2 * local + col + HEAD_DIM]
            scores = lax.dot_general(
                query, key, (((1,), (1,)), ((), ())), preferred_element_type=jnp.float32
            ) * (1.0 / math.sqrt(HEAD_DIM))
            scores = jnp.where(same, scores, -jnp.inf)
            expo = jnp.exp(scores - jnp.max(scores, axis=1, keepdims=True))
            share = 1.0 / jnp.sum(expo, axis=1, keepdims=True)
            probs = (expo * share).astype(jnp.bfloat16)
            out_ref[row : row + span, col : col + HEAD_DIM] = jnp.dot(
                probs, value, preferred_element_type=jnp.float32
            ).astype(jnp.bfloat16)


def shards(page_patches, gain, q_weight, k_weight, v_weight, pack_lengths, line_order):
    groups = lax.axis_size("dp")
    page_index = lax.axis_index("dp")
    width = page_patches.shape[1]
    slot_rows = page_patches.shape[0] // groups
    rows = slot_rows * groups // 2
    local = q_weight.shape[1]
    strip = q_weight.shape[0]
    weight = jnp.concatenate([q_weight, k_weight, v_weight], axis=1)
    weight = lax.all_gather(weight, "dp", axis=0, tiled=True, axis_index_groups=dp_groups("z"))
    targets = jnp.arange(groups, dtype=jnp.int32)
    my_order = lax.dynamic_index_in_dim(line_order, page_index, 0, keepdims=False)
    slot_for = jnp.sum(
        jnp.where(my_order[None, :] == targets[:, None], targets[None, :], 0), axis=1
    )
    slots = page_patches.reshape(groups, slot_rows, width)
    outgoing = slots.at[slot_for].get(mode="promise_in_bounds")
    outgoing, pack_lengths = lax.optimization_barrier((outgoing, pack_lengths))
    incoming = lax.all_to_all(outgoing, "dp", split_axis=0, concat_axis=0, tiled=True)
    my_lengths = lax.dynamic_index_in_dim(pack_lengths, page_index, 0, keepdims=False)
    line_ends = jnp.cumsum(my_lengths)
    line_starts = line_ends - my_lengths
    row_ids = jnp.arange(rows, dtype=jnp.int32)
    segment = jnp.sum((line_ends[None, :] <= row_ids[:, None]).astype(jnp.int32), axis=1)
    start_of_row = jnp.sum(
        jnp.where(segment[:, None] == targets[None, :], line_starts[None, :], 0), axis=1
    )
    source_rows = segment * slot_rows + row_ids - start_of_row
    packed = incoming.reshape(groups * slot_rows, width).at[source_rows].get(
        mode="promise_in_bounds"
    )

    own = jnp.concatenate([packed, jnp.broadcast_to(gain[None, :], (GAIN_ROWS, width))], axis=0)
    all_rows = rows + GAIN_ROWS
    cut = rows // 2 + GAIN_ROWS

    def along_y(block, step):
        return lax.ppermute(block, "tensor", y_shift(step))

    def along_z(block, step):
        return lax.ppermute(block, "tensor", z_shift(step))

    own_far, own_down, own_up, z_down, z_up, weight = lax.optimization_barrier(
        (
            along_y(own, 2),
            along_y(own, -1),
            along_y(own, 1),
            along_z(own, -1),
            along_z(own, 1),
            weight,
        )
    )
    weight = lax.all_gather(weight, "dp", axis=0, tiled=True, axis_index_groups=dp_groups("xc"))
    pair = jnp.concatenate([z_up, z_down], axis=0)
    pair_up, pair_down = along_y(pair, 1), along_y(pair, -1)
    pair_far_up = along_y(pair_up[:all_rows], 1)
    pair_far_down = along_y(pair_down[all_rows:], -1)
    far_top, far_rest = along_z(z_up[:cut], 1), along_z(z_down[cut:], -1)
    far_top, far_rest, pair_up, pair_down = lax.optimization_barrier(
        (far_top, far_rest, pair_up, pair_down)
    )
    far = jnp.concatenate([far_top, far_rest], axis=0)
    far_far, far_down, far_up = along_y(far, 2), along_y(far, -1), along_y(far, 1)

    blocks, slots_at, shifts = [], [], []

    def add(array, dy, *dzs):
        blocks.append(array)
        for k, dz in enumerate(dzs):
            slots_at.append((len(blocks) - 1, k * all_rows))
            shifts.append((dz, dy))

    add(own, 0, 0)
    add(own_up, -1, 0)
    add(own_down, 1, 0)
    add(own_far, 2, 0)
    add(pair, 0, -1, 1)
    add(pair_up, -1, -1, 1)
    add(pair_down, 1, -1, 1)
    add(pair_far_up, 2, -1)
    add(pair_far_down, 2, 1)
    add(far, 0, 2)
    add(far_up, -1, 2)
    add(far_down, 1, 2)
    add(far_far, 2, 2)
    tensor = lax.axis_index("tensor")
    my_z, my_y = tensor // Y_PARTS, tensor % Y_PARTS
    step_z = jnp.array([dz for dz, _ in shifts], jnp.int32)
    step_y = jnp.array([dy for _, dy in shifts], jnp.int32)
    places = (my_z + step_z + Z_PARTS) % Z_PARTS * Y_PARTS + (my_y + step_y + Y_PARTS) % Y_PARTS

    def kernel(*refs):
        project_attend_kernel(slots_at, len(blocks), rows, strip, *refs)

    features = width * len(slots_at)
    vmem = pl.BlockSpec(memory_space=pltpu.VMEM)
    smem, hbm = pl.BlockSpec(memory_space=pltpu.SMEM), pl.BlockSpec(memory_space=pl.ANY)
    return pl.pallas_call(
        kernel,
        out_shape=jax.ShapeDtypeStruct((rows, local), jnp.bfloat16),
        in_specs=[smem] + [hbm] * (len(blocks) + 1) + [vmem, vmem],
        out_specs=vmem,
        scratch_shapes=[
            pltpu.VMEM((len(slots_at), all_rows, width), jnp.bfloat16),
            pltpu.VMEM((rows, features), jnp.bfloat16),
            pltpu.VMEM((features, 3 * local), jnp.bfloat16),
            pltpu.VMEM((rows // 2, 3 * local), jnp.float32),
            pltpu.VMEM((rows, 3 * local), jnp.bfloat16),
            pltpu.SemaphoreType.DMA,
            pltpu.SemaphoreType.DMA((5,)),
        ],
        name="norm_project_attend",
    )(places, *blocks, weight, segment[:, None], segment[None, :])


def solution(mesh):
    return jax.shard_map(
        shards,
        mesh=mesh,
        in_specs=(
            P("dp", "tensor"),
            P("tensor"),
            P("dp", "tensor"),
            P("dp", "tensor"),
            P("dp", "tensor"),
            P(),
            P(),
        ),
        out_specs=P("dp", "tensor"),
        check_vma=False,
    )
```

```python
import math

import jax
import jax.numpy as jnp
from jax import lax
from jax.experimental import pallas as pl
from jax.experimental.pallas import tpu as pltpu
from jax.sharding import PartitionSpec as P

HEAD_DIM = 128
NORM_EPSILON = 1e-06
Z_PARTS, Y_PARTS = 4, 4
GAIN_ROWS = 16
ROW_TILE = 16


def z_shift(step):
    return [
        (z * Y_PARTS + y, (z + step) % Z_PARTS * Y_PARTS + y)
        for z in range(Z_PARTS)
        for y in range(Y_PARTS)
    ]


def y_shift(step):
    return [
        (z * Y_PARTS + y, z * Y_PARTS + (y + step) % Y_PARTS)
        for z in range(Z_PARTS)
        for y in range(Y_PARTS)
    ]


def dp_groups(varying):
    groups = {}
    for x in range(4):
        for z in range(4):
            for core in range(2):
                key = tuple(v for name, v in (("x", x), ("z", z), ("c", core)) if name not in varying)
                groups.setdefault(key, []).append(x * 8 + z * 2 + core)
    return list(groups.values())


def load_weights(source_ref, weight_ref, sem, strip):
    copies = []
    for x in range(4):
        for z in range(4):
            for core in range(2):
                held, wanted = (x * 2 + core) * 4 + z, x * 8 + z * 2 + core
                copies.append(
                    pltpu.make_async_copy(
                        source_ref.at[pl.ds(held * strip, strip), :],
                        weight_ref.at[pl.ds(wanted * strip, strip), :],
                        sem,
                    )
                )
    for copy in copies:
        copy.start()
    return copies


def slot_columns(places_ref, count, width):
    return [pl.ds(pl.multiple_of(places_ref[j] * width, 128), width) for j in range(count)]


def normalize(block_ref, gains, columns, row, normed_ref):
    features = normed_ref.shape[1]
    at = pl.multiple_of(row, ROW_TILE)

    def load(j):
        return block_ref[j, pl.ds(at, ROW_TILE), :].astype(jnp.float32)

    total = load(0)
    for j in range(1, len(gains)):
        total = total + load(j)
    mean = jnp.sum(total, axis=1, keepdims=True) * (1.0 / features)
    square = jnp.square(load(0) - mean)
    for j in range(1, len(gains)):
        square = square + jnp.square(load(j) - mean)
    var = jnp.sum(square, axis=1, keepdims=True) * (1.0 / features)
    scale = lax.rsqrt(var + NORM_EPSILON)
    for j in range(len(gains)):
        normed_ref[pl.ds(at, ROW_TILE), columns[j]] = (
            (load(j) - mean) * scale * gains[j]
        ).astype(jnp.bfloat16)


def project_attend_kernel(slots, count, rows, strip, *refs):
    places_ref, blocks = refs[0], refs[1 : 1 + count]
    source_ref, seg_col_ref, seg_row_ref, out_ref = refs[1 + count : 5 + count]
    block_ref, normed_ref, weight_ref, total_ref, sums_ref, sem, block_sem = refs[5 + count :]
    width, features = block_ref.shape[2], normed_ref.shape[1]
    half = rows // 2
    parts = [(rows, GAIN_ROWS)] + [(row, rows // 4) for row in range(0, rows, rows // 4)]
    block_copies = []
    for k, (row, size) in enumerate(parts):
        block_copies.append(
            [
                pltpu.make_async_copy(
                    blocks[ref].at[pl.ds(start + row, size), :],
                    block_ref.at[j, pl.ds(row, size), :],
                    block_sem.at[k],
                )
                for j, (ref, start) in enumerate(slots)
            ]
        )
    for copies in block_copies:
        for copy in copies:
            copy.start()
    weight_copies = load_weights(source_ref, weight_ref, sem, strip)
    columns = slot_columns(places_ref, len(slots), width)
    for copy in block_copies[0]:
        copy.wait()
    gains = [
        block_ref[j, pl.ds(rows, GAIN_ROWS), :][:1].astype(jnp.float32) for j in range(len(slots))
    ]

    for k in range(2):
        for copy in block_copies[1 + k]:
            copy.wait()

        def first_step(i, carry):
            normalize(block_ref, gains, columns, k * rows // 4 + i * ROW_TILE, normed_ref)
            return carry

        lax.fori_loop(0, rows // 4 // ROW_TILE, first_step, 0)

    for copies in (block_copies[3], block_copies[4], weight_copies):
        for copy in copies:
            copy.wait()
    steps = half // (2 * ROW_TILE)
    depth = features // steps
    total_ref[...] = jnp.zeros_like(total_ref)

    def second_step(i, carry):
        at = pl.ds(pl.multiple_of(i * depth, depth), depth)
        total_ref[...] += jnp.dot(
            normed_ref[:half, at], weight_ref[at, :], preferred_element_type=jnp.float32
        )
        for k in range(2):
            normalize(block_ref, gains, columns, half + (2 * i + k) * ROW_TILE, normed_ref)
        return carry

    lax.fori_loop(0, steps, second_step, 0)
    sums_ref[:half] = total_ref[...].astype(jnp.bfloat16)
    sums_ref[half:] = jnp.dot(
        normed_ref[half:], weight_ref[...], preferred_element_type=jnp.float32
    ).astype(jnp.bfloat16)
    local = out_ref.shape[1]
    span, window = 128, 256
    for row in range(0, rows, span):
        low = min(max(row - (window - span) // 2, 0), rows - window)
        same = seg_col_ref[row : row + span, :1] == seg_row_ref[:1, low : low + window]
        for col in range(0, local, HEAD_DIM):
            query = sums_ref[row : row + span, col : col + HEAD_DIM]
            key = sums_ref[low : low + window, local + col : local + col + HEAD_DIM]
            value = sums_ref[low : low + window, 2 * local + col : 2 * local + col + HEAD_DIM]
            scores = lax.dot_general(
                query, key, (((1,), (1,)), ((), ())), preferred_element_type=jnp.float32
            ) * (1.0 / math.sqrt(HEAD_DIM))
            scores = jnp.where(same, scores, -jnp.inf)
            expo = jnp.exp(scores - jnp.max(scores, axis=1, keepdims=True))
            share = 1.0 / jnp.sum(expo, axis=1, keepdims=True)
            probs = (expo * share).astype(jnp.bfloat16)
            out_ref[row : row + span, col : col + HEAD_DIM] = jnp.dot(
                probs, value, preferred_element_type=jnp.float32
            ).astype(jnp.bfloat16)


def shards(page_patches, gain, q_weight, k_weight, v_weight, pack_lengths, line_order):
    groups = lax.axis_size("dp")
    page_index = lax.axis_index("dp")
    width = page_patches.shape[1]
    slot_rows = page_patches.shape[0] // groups
    rows = slot_rows * groups // 2
    local = q_weight.shape[1]
    strip = q_weight.shape[0]
    weight = jnp.concatenate([q_weight, k_weight, v_weight], axis=1)
    weight = lax.all_gather(weight, "dp", axis=0, tiled=True, axis_index_groups=dp_groups("z"))
    targets = jnp.arange(groups, dtype=jnp.int32)
    my_order = lax.dynamic_index_in_dim(line_order, page_index, 0, keepdims=False)
    slot_for = jnp.sum(
        jnp.where(my_order[None, :] == targets[:, None], targets[None, :], 0), axis=1
    )
    slots = page_patches.reshape(groups, slot_rows, width)
    outgoing = slots.at[slot_for].get(mode="promise_in_bounds")
    outgoing, pack_lengths = lax.optimization_barrier((outgoing, pack_lengths))
    incoming = lax.all_to_all(outgoing, "dp", split_axis=0, concat_axis=0, tiled=True)
    my_lengths = lax.dynamic_index_in_dim(pack_lengths, page_index, 0, keepdims=False)
    line_ends = jnp.cumsum(my_lengths)
    line_starts = line_ends - my_lengths
    row_ids = jnp.arange(rows, dtype=jnp.int32)
    segment = jnp.sum((line_ends[None, :] <= row_ids[:, None]).astype(jnp.int32), axis=1)
    start_of_row = jnp.sum(
        jnp.where(segment[:, None] == targets[None, :], line_starts[None, :], 0), axis=1
    )
    source_rows = segment * slot_rows + row_ids - start_of_row
    packed = incoming.reshape(groups * slot_rows, width).at[source_rows].get(
        mode="promise_in_bounds"
    )

    own = jnp.concatenate([packed, jnp.broadcast_to(gain[None, :], (GAIN_ROWS, width))], axis=0)
    all_rows = rows + GAIN_ROWS
    cut = rows // 2 + GAIN_ROWS

    def along_y(block, step):
        return lax.ppermute(block, "tensor", y_shift(step))

    def along_z(block, step):
        return lax.ppermute(block, "tensor", z_shift(step))

    z_up, z_down, own_up, own_down, own_far, weight = lax.optimization_barrier(
        (
            along_z(own, 1),
            along_z(own, -1),
            along_y(own, 1),
            along_y(own, -1),
            along_y(own, 2),
            weight,
        )
    )
    weight = lax.all_gather(weight, "dp", axis=0, tiled=True, axis_index_groups=dp_groups("xc"))
    pair = jnp.concatenate([z_up, z_down], axis=0)
    pair_up, pair_down = along_y(pair, 1), along_y(pair, -1)
    pair_far_up = along_y(pair_up[:all_rows], 1)
    pair_far_down = along_y(pair_down[all_rows:], -1)
    far_top, far_rest = along_z(z_up[:cut], 1), along_z(z_down[cut:], -1)
    far = jnp.concatenate([far_top, far_rest], axis=0)
    far_all = lax.all_to_all(
        jnp.broadcast_to(far[None], (Y_PARTS, *far.shape)),
        "tensor",
        split_axis=0,
        concat_axis=0,
        tiled=True,
        axis_index_groups=[[z * Y_PARTS + y for y in range(Y_PARTS)] for z in range(Z_PARTS)],
    )

    blocks, slots_at, shifts = [], [], []

    def add(array, dy, *dzs):
        blocks.append(array)
        for k, dz in enumerate(dzs):
            slots_at.append((len(blocks) - 1, k * all_rows))
            shifts.append((dz, dy))

    add(own, 0, 0)
    add(own_up, -1, 0)
    add(own_down, 1, 0)
    add(own_far, 2, 0)
    add(pair, 0, -1, 1)
    add(pair_up, -1, -1, 1)
    add(pair_down, 1, -1, 1)
    add(pair_far_up, 2, -1)
    add(pair_far_down, 2, 1)
    blocks.append(far_all.reshape(Y_PARTS * all_rows, width))
    for y in range(Y_PARTS):
        slots_at.append((len(blocks) - 1, y * all_rows))
    tensor = lax.axis_index("tensor")
    my_z, my_y = tensor // Y_PARTS, tensor % Y_PARTS
    step_z = jnp.array([dz for dz, _ in shifts] + [2] * Y_PARTS, jnp.int32)
    step_y = jnp.array([dy for _, dy in shifts], jnp.int32)
    step_y = jnp.concatenate([step_y, jnp.arange(Y_PARTS, dtype=jnp.int32) - my_y])
    places = (my_z + step_z + Z_PARTS) % Z_PARTS * Y_PARTS + (my_y + step_y + Y_PARTS) % Y_PARTS

    def kernel(*refs):
        project_attend_kernel(slots_at, len(blocks), rows, strip, *refs)

    features = width * len(slots_at)
    vmem = pl.BlockSpec(memory_space=pltpu.VMEM)
    smem, hbm = pl.BlockSpec(memory_space=pltpu.SMEM), pl.BlockSpec(memory_space=pl.ANY)
    return pl.pallas_call(
        kernel,
        out_shape=jax.ShapeDtypeStruct((rows, local), jnp.bfloat16),
        in_specs=[smem] + [hbm] * (len(blocks) + 1) + [vmem, vmem],
        out_specs=vmem,
        scratch_shapes=[
            pltpu.VMEM((len(slots_at), all_rows, width), jnp.bfloat16),
            pltpu.VMEM((rows, features), jnp.bfloat16),
            pltpu.VMEM((features, 3 * local), jnp.bfloat16),
            pltpu.VMEM((rows // 2, 3 * local), jnp.float32),
            pltpu.VMEM((rows, 3 * local), jnp.bfloat16),
            pltpu.SemaphoreType.DMA,
            pltpu.SemaphoreType.DMA((5,)),
        ],
        name="norm_project_attend",
    )(places, *blocks, weight, segment[:, None], segment[None, :])


def solution(mesh):
    return jax.shard_map(
        shards,
        mesh=mesh,
        in_specs=(
            P("dp", "tensor"),
            P("tensor"),
            P("dp", "tensor"),
            P("dp", "tensor"),
            P("dp", "tensor"),
            P(),
            P(),
        ),
        out_specs=P("dp", "tensor"),
        check_vma=False,
    )
```

```python
import math

import jax
import jax.numpy as jnp
from jax import lax
from jax.experimental import pallas as pl
from jax.experimental.pallas import tpu as pltpu
from jax.sharding import PartitionSpec as P

HEAD_DIM = 128
NORM_EPSILON = 1e-06
Z_PARTS, Y_PARTS = 4, 4
GAIN_ROWS = 16
ROW_TILE = 16


def z_shift(step):
    return [
        (z * Y_PARTS + y, (z + step) % Z_PARTS * Y_PARTS + y)
        for z in range(Z_PARTS)
        for y in range(Y_PARTS)
    ]


def y_shift(step):
    return [
        (z * Y_PARTS + y, z * Y_PARTS + (y + step) % Y_PARTS)
        for z in range(Z_PARTS)
        for y in range(Y_PARTS)
    ]


def dp_groups(varying):
    groups = {}
    for x in range(4):
        for z in range(4):
            for core in range(2):
                key = tuple(v for name, v in (("x", x), ("z", z), ("c", core)) if name not in varying)
                groups.setdefault(key, []).append(x * 8 + z * 2 + core)
    return list(groups.values())


def load_weights(source_ref, weight_ref, sem, strip):
    copies = []
    for x in range(4):
        for z in range(4):
            for core in range(2):
                held, wanted = (x * 2 + core) * 4 + z, x * 8 + z * 2 + core
                copies.append(
                    pltpu.make_async_copy(
                        source_ref.at[pl.ds(held * strip, strip), :],
                        weight_ref.at[pl.ds(wanted * strip, strip), :],
                        sem,
                    )
                )
    for copy in copies:
        copy.start()
    return copies


def slot_columns(places_ref, count, width):
    return [pl.ds(pl.multiple_of(places_ref[j] * width, 128), width) for j in range(count)]


def normalize(block_ref, gains, columns, row, normed_ref):
    features = normed_ref.shape[1]
    at = pl.multiple_of(row, ROW_TILE)

    def load(j):
        return block_ref[j, pl.ds(at, ROW_TILE), :].astype(jnp.float32)

    total = load(0)
    for j in range(1, len(gains)):
        total = total + load(j)
    mean = jnp.sum(total, axis=1, keepdims=True) * (1.0 / features)
    square = jnp.square(load(0) - mean)
    for j in range(1, len(gains)):
        square = square + jnp.square(load(j) - mean)
    var = jnp.sum(square, axis=1, keepdims=True) * (1.0 / features)
    scale = lax.rsqrt(var + NORM_EPSILON)
    for j in range(len(gains)):
        normed_ref[pl.ds(at, ROW_TILE), columns[j]] = (
            (load(j) - mean) * scale * gains[j]
        ).astype(jnp.bfloat16)


def project_attend_kernel(slots, count, rows, strip, *refs):
    places_ref, blocks = refs[0], refs[1 : 1 + count]
    source_ref, seg_col_ref, seg_row_ref, out_ref = refs[1 + count : 5 + count]
    block_ref, normed_ref, weight_ref, total_ref, sums_ref, sem, block_sem = refs[5 + count :]
    width, features = block_ref.shape[2], normed_ref.shape[1]
    half = rows // 2
    parts = [(rows, GAIN_ROWS)] + [(row, rows // 4) for row in range(0, rows, rows // 4)]
    block_copies = []
    for k, (row, size) in enumerate(parts):
        block_copies.append(
            [
                pltpu.make_async_copy(
                    blocks[ref].at[pl.ds(start + row, size), :],
                    block_ref.at[j, pl.ds(row, size), :],
                    block_sem.at[k],
                )
                for j, (ref, start) in enumerate(slots)
            ]
        )
    for copies in block_copies:
        for copy in copies:
            copy.start()
    weight_copies = load_weights(source_ref, weight_ref, sem, strip)
    columns = slot_columns(places_ref, len(slots), width)
    for copy in block_copies[0]:
        copy.wait()
    gains = [
        block_ref[j, pl.ds(rows, GAIN_ROWS), :][:1].astype(jnp.float32) for j in range(len(slots))
    ]

    for k in range(2):
        for copy in block_copies[1 + k]:
            copy.wait()

        def first_step(i, carry):
            normalize(block_ref, gains, columns, k * rows // 4 + i * ROW_TILE, normed_ref)
            return carry

        lax.fori_loop(0, rows // 4 // ROW_TILE, first_step, 0)

    for copies in (block_copies[3], block_copies[4], weight_copies):
        for copy in copies:
            copy.wait()
    steps = half // (2 * ROW_TILE)
    depth = features // steps
    total_ref[...] = jnp.zeros_like(total_ref)

    def second_step(i, carry):
        at = pl.ds(pl.multiple_of(i * depth, depth), depth)
        total_ref[...] += jnp.dot(
            normed_ref[:half, at], weight_ref[at, :], preferred_element_type=jnp.float32
        )
        for k in range(2):
            normalize(block_ref, gains, columns, half + (2 * i + k) * ROW_TILE, normed_ref)
        return carry

    lax.fori_loop(0, steps, second_step, 0)
    sums_ref[:half] = total_ref[...].astype(jnp.bfloat16)
    sums_ref[half:] = jnp.dot(
        normed_ref[half:], weight_ref[...], preferred_element_type=jnp.float32
    ).astype(jnp.bfloat16)
    local = out_ref.shape[1]
    span, window = 64, 128
    for row in range(0, rows, span):
        low = min(max(row - (window - span) // 2, 0), rows - window)
        same = seg_col_ref[row : row + span, :1] == seg_row_ref[:1, low : low + window]
        for col in range(0, local, HEAD_DIM):
            query = sums_ref[row : row + span, col : col + HEAD_DIM]
            key = sums_ref[low : low + window, local + col : local + col + HEAD_DIM]
            value = sums_ref[low : low + window, 2 * local + col : 2 * local + col + HEAD_DIM]
            scores = lax.dot_general(
                query, key, (((1,), (1,)), ((), ())), preferred_element_type=jnp.float32
            ) * (1.0 / math.sqrt(HEAD_DIM))
            scores = jnp.where(same, scores, -jnp.inf)
            expo = jnp.exp(scores - jnp.max(scores, axis=1, keepdims=True))
            share = 1.0 / jnp.sum(expo, axis=1, keepdims=True)
            probs = (expo * share).astype(jnp.bfloat16)
            out_ref[row : row + span, col : col + HEAD_DIM] = jnp.dot(
                probs, value, preferred_element_type=jnp.float32
            ).astype(jnp.bfloat16)


def shards(page_patches, gain, q_weight, k_weight, v_weight, pack_lengths, line_order):
    groups = lax.axis_size("dp")
    page_index = lax.axis_index("dp")
    width = page_patches.shape[1]
    slot_rows = page_patches.shape[0] // groups
    rows = slot_rows * groups // 2
    local = q_weight.shape[1]
    strip = q_weight.shape[0]
    weight = jnp.concatenate([q_weight, k_weight, v_weight], axis=1)
    weight = lax.all_gather(weight, "dp", axis=0, tiled=True, axis_index_groups=dp_groups("z"))
    targets = jnp.arange(groups, dtype=jnp.int32)
    my_order = lax.dynamic_index_in_dim(line_order, page_index, 0, keepdims=False)
    slot_for = jnp.sum(
        jnp.where(my_order[None, :] == targets[:, None], targets[None, :], 0), axis=1
    )
    slots = page_patches.reshape(groups, slot_rows, width)
    outgoing = slots.at[slot_for].get(mode="promise_in_bounds")
    outgoing, pack_lengths = lax.optimization_barrier((outgoing, pack_lengths))
    incoming = lax.all_to_all(outgoing, "dp", split_axis=0, concat_axis=0, tiled=True)
    my_lengths = lax.dynamic_index_in_dim(pack_lengths, page_index, 0, keepdims=False)
    line_ends = jnp.cumsum(my_lengths)
    line_starts = line_ends - my_lengths
    row_ids = jnp.arange(rows, dtype=jnp.int32)
    segment = jnp.sum((line_ends[None, :] <= row_ids[:, None]).astype(jnp.int32), axis=1)
    start_of_row = jnp.sum(
        jnp.where(segment[:, None] == targets[None, :], line_starts[None, :], 0), axis=1
    )
    source_rows = segment * slot_rows + row_ids - start_of_row
    packed = incoming.reshape(groups * slot_rows, width).at[source_rows].get(
        mode="promise_in_bounds"
    )

    own = jnp.concatenate([packed, jnp.broadcast_to(gain[None, :], (GAIN_ROWS, width))], axis=0)
    all_rows = rows + GAIN_ROWS
    cut = rows // 2 + GAIN_ROWS

    def along_y(block, step):
        return lax.ppermute(block, "tensor", y_shift(step))

    def along_z(block, step):
        return lax.ppermute(block, "tensor", z_shift(step))

    z_up, z_down, own_up, own_down, own_far, weight = lax.optimization_barrier(
        (
            along_z(own, 1),
            along_z(own, -1),
            along_y(own, 1),
            along_y(own, -1),
            along_y(own, 2),
            weight,
        )
    )
    weight = lax.all_gather(weight, "dp", axis=0, tiled=True, axis_index_groups=dp_groups("xc"))
    pair = jnp.concatenate([z_up, z_down], axis=0)
    pair_up, pair_down = along_y(pair, 1), along_y(pair, -1)
    pair_far_up = along_y(pair_up[:all_rows], 1)
    pair_far_down = along_y(pair_down[all_rows:], -1)
    far_top, far_rest = along_z(z_up[:cut], 1), along_z(z_down[cut:], -1)
    far_top, far_rest, pair_up, pair_down = lax.optimization_barrier(
        (far_top, far_rest, pair_up, pair_down)
    )
    far = jnp.concatenate([far_top, far_rest], axis=0)
    far_all = lax.all_to_all(
        jnp.broadcast_to(far[None], (Y_PARTS, *far.shape)),
        "tensor",
        split_axis=0,
        concat_axis=0,
        tiled=True,
        axis_index_groups=[[z * Y_PARTS + y for y in range(Y_PARTS)] for z in range(Z_PARTS)],
    )

    blocks, slots_at, shifts = [], [], []

    def add(array, dy, *dzs):
        blocks.append(array)
        for k, dz in enumerate(dzs):
            slots_at.append((len(blocks) - 1, k * all_rows))
            shifts.append((dz, dy))

    add(own, 0, 0)
    add(own_up, -1, 0)
    add(own_down, 1, 0)
    add(own_far, 2, 0)
    add(pair, 0, -1, 1)
    add(pair_up, -1, -1, 1)
    add(pair_down, 1, -1, 1)
    add(pair_far_up, 2, -1)
    add(pair_far_down, 2, 1)
    blocks.append(far_all.reshape(Y_PARTS * all_rows, width))
    for y in range(Y_PARTS):
        slots_at.append((len(blocks) - 1, y * all_rows))
    tensor = lax.axis_index("tensor")
    my_z, my_y = tensor // Y_PARTS, tensor % Y_PARTS
    step_z = jnp.array([dz for dz, _ in shifts] + [2] * Y_PARTS, jnp.int32)
    step_y = jnp.array([dy for _, dy in shifts], jnp.int32)
    step_y = jnp.concatenate([step_y, jnp.arange(Y_PARTS, dtype=jnp.int32) - my_y])
    places = (my_z + step_z + Z_PARTS) % Z_PARTS * Y_PARTS + (my_y + step_y + Y_PARTS) % Y_PARTS

    def kernel(*refs):
        project_attend_kernel(slots_at, len(blocks), rows, strip, *refs)

    features = width * len(slots_at)
    vmem = pl.BlockSpec(memory_space=pltpu.VMEM)
    smem, hbm = pl.BlockSpec(memory_space=pltpu.SMEM), pl.BlockSpec(memory_space=pl.ANY)
    return pl.pallas_call(
        kernel,
        out_shape=jax.ShapeDtypeStruct((rows, local), jnp.bfloat16),
        in_specs=[smem] + [hbm] * (len(blocks) + 1) + [vmem, vmem],
        out_specs=vmem,
        scratch_shapes=[
            pltpu.VMEM((len(slots_at), all_rows, width), jnp.bfloat16),
            pltpu.VMEM((rows, features), jnp.bfloat16),
            pltpu.VMEM((features, 3 * local), jnp.bfloat16),
            pltpu.VMEM((rows // 2, 3 * local), jnp.float32),
            pltpu.VMEM((rows, 3 * local), jnp.bfloat16),
            pltpu.SemaphoreType.DMA,
            pltpu.SemaphoreType.DMA((5,)),
        ],
        name="norm_project_attend",
    )(places, *blocks, weight, segment[:, None], segment[None, :])


def solution(mesh):
    return jax.shard_map(
        shards,
        mesh=mesh,
        in_specs=(
            P("dp", "tensor"),
            P("tensor"),
            P("dp", "tensor"),
            P("dp", "tensor"),
            P("dp", "tensor"),
            P(),
            P(),
        ),
        out_specs=P("dp", "tensor"),
        check_vma=False,
    )
```

```python
import math

import jax
import jax.numpy as jnp
from jax import lax
from jax.experimental import pallas as pl
from jax.experimental.pallas import tpu as pltpu
from jax.sharding import PartitionSpec as P

HEAD_DIM = 128
NORM_EPSILON = 1e-06
Z_PARTS, Y_PARTS = 4, 4
ROW_TILE = 16


def z_shift(step):
    return [
        (z * Y_PARTS + y, (z + step) % Z_PARTS * Y_PARTS + y)
        for z in range(Z_PARTS)
        for y in range(Y_PARTS)
    ]


def y_shift(step):
    return [
        (z * Y_PARTS + y, z * Y_PARTS + (y + step) % Y_PARTS)
        for z in range(Z_PARTS)
        for y in range(Y_PARTS)
    ]


def dp_groups(varying):
    groups = {}
    for x in range(4):
        for z in range(4):
            for core in range(2):
                key = tuple(v for name, v in (("x", x), ("z", z), ("c", core)) if name not in varying)
                groups.setdefault(key, []).append(x * 8 + z * 2 + core)
    return list(groups.values())


def load_weights(source_ref, weight_ref, sem, strip):
    copies = []
    for x in range(4):
        for z in range(4):
            for core in range(2):
                held, wanted = (x * 2 + core) * 4 + z, x * 8 + z * 2 + core
                copies.append(
                    pltpu.make_async_copy(
                        source_ref.at[pl.ds(held * strip, strip), :],
                        weight_ref.at[pl.ds(wanted * strip, strip), :],
                        sem,
                    )
                )
    for copy in copies:
        copy.start()
    return copies


def slot_columns(places_ref, count, width):
    return [pl.ds(pl.multiple_of(places_ref[j] * width, 128), width) for j in range(count)]


def normalize(block_ref, gains, columns, row, normed_ref):
    features = normed_ref.shape[1]
    at = pl.multiple_of(row, ROW_TILE)

    def load(j):
        return block_ref[j, pl.ds(at, ROW_TILE), :].astype(jnp.float32)

    total = load(0)
    for j in range(1, len(gains)):
        total = total + load(j)
    mean = jnp.sum(total, axis=1, keepdims=True) * (1.0 / features)
    square = jnp.square(load(0) - mean)
    for j in range(1, len(gains)):
        square = square + jnp.square(load(j) - mean)
    var = jnp.sum(square, axis=1, keepdims=True) * (1.0 / features)
    scale = lax.rsqrt(var + NORM_EPSILON)
    for j in range(len(gains)):
        normed_ref[pl.ds(at, ROW_TILE), columns[j]] = (
            (load(j) - mean) * scale * gains[j]
        ).astype(jnp.bfloat16)


def project_attend_kernel(slots, count, rows, strip, *refs):
    places_ref, blocks = refs[0], refs[1 : 1 + count]
    source_ref, gain_ref, seg_col_ref, seg_row_ref, out_ref = refs[1 + count : 6 + count]
    block_ref, normed_ref, weight_ref, total_ref, sums_ref, sem, block_sem = refs[6 + count :]
    width, features = block_ref.shape[2], normed_ref.shape[1]
    half = rows // 2
    parts = [(row, rows // 4) for row in range(0, rows, rows // 4)]
    block_copies = []
    for k, (row, size) in enumerate(parts):
        block_copies.append(
            [
                pltpu.make_async_copy(
                    blocks[ref].at[pl.ds(start + row, size), :],
                    block_ref.at[j, pl.ds(row, size), :],
                    block_sem.at[k],
                )
                for j, (ref, start) in enumerate(slots)
            ]
        )
    for copies in block_copies:
        for copy in copies:
            copy.start()
    weight_copies = load_weights(source_ref, weight_ref, sem, strip)
    columns = slot_columns(places_ref, len(slots), width)
    gains = [gain_ref[pl.ds(places_ref[j], 1), :] for j in range(len(slots))]

    for k in range(2):
        for copy in block_copies[k]:
            copy.wait()

        def first_step(i, carry):
            normalize(block_ref, gains, columns, k * rows // 4 + i * ROW_TILE, normed_ref)
            return carry

        lax.fori_loop(0, rows // 4 // ROW_TILE, first_step, 0)

    for copies in (block_copies[2], block_copies[3], weight_copies):
        for copy in copies:
            copy.wait()
    steps = half // (2 * ROW_TILE)
    depth = features // steps
    total_ref[...] = jnp.zeros_like(total_ref)

    def second_step(i, carry):
        at = pl.ds(pl.multiple_of(i * depth, depth), depth)
        total_ref[...] += jnp.dot(
            normed_ref[:half, at], weight_ref[at, :], preferred_element_type=jnp.float32
        )
        for k in range(2):
            normalize(block_ref, gains, columns, half + (2 * i + k) * ROW_TILE, normed_ref)
        return carry

    lax.fori_loop(0, steps, second_step, 0)
    sums_ref[:half] = total_ref[...].astype(jnp.bfloat16)
    sums_ref[half:] = jnp.dot(
        normed_ref[half:], weight_ref[...], preferred_element_type=jnp.float32
    ).astype(jnp.bfloat16)
    local = out_ref.shape[1]
    span, window = 128, 256
    for row in range(0, rows, span):
        low = min(max(row - (window - span) // 2, 0), rows - window)
        same = seg_col_ref[row : row + span, :1] == seg_row_ref[:1, low : low + window]
        heads = range(0, local, HEAD_DIM)
        scores = [
            lax.dot_general(
                sums_ref[row : row + span, col : col + HEAD_DIM],
                sums_ref[low : low + window, local + col : local + col + HEAD_DIM],
                (((1,), (1,)), ((), ())),
                preferred_element_type=jnp.float32,
            )
            * (1.0 / math.sqrt(HEAD_DIM))
            for col in heads
        ]
        scores = [jnp.where(same, one, -jnp.inf) for one in scores]
        tops = [jnp.max(one, axis=1, keepdims=True) for one in scores]
        expos = [jnp.exp(one - top) for one, top in zip(scores, tops)]
        shares = [1.0 / jnp.sum(expo, axis=1, keepdims=True) for expo in expos]
        for col, expo, share in zip(heads, expos, shares):
            value = sums_ref[low : low + window, 2 * local + col : 2 * local + col + HEAD_DIM]
            out_ref[row : row + span, col : col + HEAD_DIM] = jnp.dot(
                (expo * share).astype(jnp.bfloat16), value, preferred_element_type=jnp.float32
            ).astype(jnp.bfloat16)


def shards(page_patches, gain, q_weight, k_weight, v_weight, pack_lengths, line_order):
    groups = lax.axis_size("dp")
    page_index = lax.axis_index("dp")
    width = page_patches.shape[1]
    slot_rows = page_patches.shape[0] // groups
    rows = slot_rows * groups // 2
    local = q_weight.shape[1]
    strip = q_weight.shape[0]
    weight = jnp.concatenate([q_weight, k_weight, v_weight], axis=1)
    weight = lax.all_gather(weight, "dp", axis=0, tiled=True, axis_index_groups=dp_groups("z"))
    targets = jnp.arange(groups, dtype=jnp.int32)
    my_order = lax.dynamic_index_in_dim(line_order, page_index, 0, keepdims=False)
    slot_for = jnp.sum(
        jnp.where(my_order[None, :] == targets[:, None], targets[None, :], 0), axis=1
    )
    slots = page_patches.reshape(groups, slot_rows, width)
    outgoing = slots.at[slot_for].get(mode="promise_in_bounds")
    outgoing, pack_lengths = lax.optimization_barrier((outgoing, pack_lengths))
    incoming = lax.all_to_all(outgoing, "dp", split_axis=0, concat_axis=0, tiled=True)
    my_lengths = lax.dynamic_index_in_dim(pack_lengths, page_index, 0, keepdims=False)
    line_ends = jnp.cumsum(my_lengths)
    line_starts = line_ends - my_lengths
    row_ids = jnp.arange(rows, dtype=jnp.int32)
    segment = jnp.sum((line_ends[None, :] <= row_ids[:, None]).astype(jnp.int32), axis=1)
    start_of_row = jnp.sum(
        jnp.where(segment[:, None] == targets[None, :], line_starts[None, :], 0), axis=1
    )
    source_rows = segment * slot_rows + row_ids - start_of_row
    packed = incoming.reshape(groups * slot_rows, width).at[source_rows].get(
        mode="promise_in_bounds"
    )

    own, cut = packed, rows // 2
    features = width * Y_PARTS * Z_PARTS
    all_gain = jnp.broadcast_to(gain[None, :], (features // width, width))
    all_gain = lax.all_to_all(all_gain, "tensor", 0, 0, tiled=True)

    def along_y(block, step):
        return lax.ppermute(block, "tensor", y_shift(step))

    def along_z(block, step):
        return lax.ppermute(block, "tensor", z_shift(step))

    z_up, z_down, own_up, own_down, own_far, all_gain, weight = lax.optimization_barrier(
        (
            along_z(own, 1),
            along_z(own, -1),
            along_y(own, 1),
            along_y(own, -1),
            along_y(own, 2),
            all_gain,
            weight,
        )
    )
    weight = lax.all_gather(weight, "dp", axis=0, tiled=True, axis_index_groups=dp_groups("xc"))
    pair = jnp.concatenate([z_up, z_down], axis=0)
    pair_up, pair_down = along_y(pair, 1), along_y(pair, -1)
    pair_far_up = along_y(pair_up[:rows], 1)
    pair_far_down = along_y(pair_down[rows:], -1)
    far_top, far_rest = along_z(z_up[:cut], 1), along_z(z_down[cut:], -1)
    far = jnp.concatenate([far_top, far_rest], axis=0)
    far_all = lax.all_to_all(
        jnp.broadcast_to(far[None], (Y_PARTS, *far.shape)),
        "tensor",
        split_axis=0,
        concat_axis=0,
        tiled=True,
        axis_index_groups=[[z * Y_PARTS + y for y in range(Y_PARTS)] for z in range(Z_PARTS)],
    )

    blocks, slots_at, shifts = [], [], []

    def add(array, dy, *dzs):
        blocks.append(array)
        for k, dz in enumerate(dzs):
            slots_at.append((len(blocks) - 1, k * rows))
            shifts.append((dz, dy))

    add(own, 0, 0)
    add(own_up, -1, 0)
    add(own_down, 1, 0)
    add(own_far, 2, 0)
    add(pair, 0, -1, 1)
    add(pair_up, -1, -1, 1)
    add(pair_down, 1, -1, 1)
    add(pair_far_up, 2, -1)
    add(pair_far_down, 2, 1)
    blocks.append(far_all.reshape(Y_PARTS * rows, width))
    for y in range(Y_PARTS):
        slots_at.append((len(blocks) - 1, y * rows))
    tensor = lax.axis_index("tensor")
    my_z, my_y = tensor // Y_PARTS, tensor % Y_PARTS
    step_z = jnp.array([dz for dz, _ in shifts] + [2] * Y_PARTS, jnp.int32)
    step_y = jnp.array([dy for _, dy in shifts], jnp.int32)
    step_y = jnp.concatenate([step_y, jnp.arange(Y_PARTS, dtype=jnp.int32) - my_y])
    places = (my_z + step_z + Z_PARTS) % Z_PARTS * Y_PARTS + (my_y + step_y + Y_PARTS) % Y_PARTS

    def kernel(*refs):
        project_attend_kernel(slots_at, len(blocks), rows, strip, *refs)

    vmem = pl.BlockSpec(memory_space=pltpu.VMEM)
    smem, hbm = pl.BlockSpec(memory_space=pltpu.SMEM), pl.BlockSpec(memory_space=pl.ANY)
    return pl.pallas_call(
        kernel,
        out_shape=jax.ShapeDtypeStruct((rows, local), jnp.bfloat16),
        in_specs=[smem] + [hbm] * (len(blocks) + 1) + [vmem] * 3,
        out_specs=vmem,
        scratch_shapes=[
            pltpu.VMEM((len(slots_at), rows, width), jnp.bfloat16),
            pltpu.VMEM((rows, features), jnp.bfloat16),
            pltpu.VMEM((features, 3 * local), jnp.bfloat16),
            pltpu.VMEM((rows // 2, 3 * local), jnp.float32),
            pltpu.VMEM((rows, 3 * local), jnp.bfloat16),
            pltpu.SemaphoreType.DMA,
            pltpu.SemaphoreType.DMA((4,)),
        ],
        name="norm_project_attend",
    )(places, *blocks, weight, all_gain.astype(jnp.float32), segment[:, None], segment[None, :])


def solution(mesh):
    return jax.shard_map(
        shards,
        mesh=mesh,
        in_specs=(
            P("dp", "tensor"),
            P("tensor"),
            P("dp", "tensor"),
            P("dp", "tensor"),
            P("dp", "tensor"),
            P(),
            P(),
        ),
        out_specs=P("dp", "tensor"),
        check_vma=False,
    )
```

```python
import math

import jax
import jax.numpy as jnp
from jax import lax
from jax.experimental import pallas as pl
from jax.experimental.pallas import tpu as pltpu
from jax.sharding import PartitionSpec as P

HEAD_DIM = 128
NORM_EPSILON = 1e-06
Z_PARTS, Y_PARTS = 4, 4
GAIN_ROWS = 16
ROW_TILE = 16


def z_shift(step):
    return [
        (z * Y_PARTS + y, (z + step) % Z_PARTS * Y_PARTS + y)
        for z in range(Z_PARTS)
        for y in range(Y_PARTS)
    ]


def y_shift(step):
    return [
        (z * Y_PARTS + y, z * Y_PARTS + (y + step) % Y_PARTS)
        for z in range(Z_PARTS)
        for y in range(Y_PARTS)
    ]


def dp_groups(varying):
    groups = {}
    for x in range(4):
        for z in range(4):
            for core in range(2):
                key = tuple(v for name, v in (("x", x), ("z", z), ("c", core)) if name not in varying)
                groups.setdefault(key, []).append(x * 8 + z * 2 + core)
    return list(groups.values())


def load_weights(source_ref, weight_ref, sem, strip):
    copies = []
    for x in range(4):
        for z in range(4):
            for core in range(2):
                held, wanted = (x * 2 + core) * 4 + z, x * 8 + z * 2 + core
                copies.append(
                    pltpu.make_async_copy(
                        source_ref.at[pl.ds(held * strip, strip), :],
                        weight_ref.at[pl.ds(wanted * strip, strip), :],
                        sem,
                    )
                )
    for copy in copies:
        copy.start()
    return copies


def slot_columns(places_ref, count, width):
    return [pl.ds(pl.multiple_of(places_ref[j] * width, 128), width) for j in range(count)]


def normalize(block_ref, gains, columns, row, normed_ref):
    features = normed_ref.shape[1]
    at = pl.multiple_of(row, ROW_TILE)

    def load(j):
        return block_ref[j, pl.ds(at, ROW_TILE), :].astype(jnp.float32)

    total = load(0)
    for j in range(1, len(gains)):
        total = total + load(j)
    mean = jnp.sum(total, axis=1, keepdims=True) * (1.0 / features)
    square = jnp.square(load(0) - mean)
    for j in range(1, len(gains)):
        square = square + jnp.square(load(j) - mean)
    var = jnp.sum(square, axis=1, keepdims=True) * (1.0 / features)
    scale = lax.rsqrt(var + NORM_EPSILON)
    for j in range(len(gains)):
        normed_ref[pl.ds(at, ROW_TILE), columns[j]] = (
            (load(j) - mean) * scale * gains[j]
        ).astype(jnp.bfloat16)


def project_attend_kernel(slots, count, rows, strip, *refs):
    places_ref, blocks = refs[0], refs[1 : 1 + count]
    source_ref, seg_col_ref, seg_row_ref, out_ref = refs[1 + count : 5 + count]
    block_ref, normed_ref, weight_ref, total_ref, sums_ref, sem, block_sem = refs[5 + count :]
    width, features = block_ref.shape[2], normed_ref.shape[1]
    half = rows // 2
    parts = [(rows, GAIN_ROWS)] + [(row, rows // 4) for row in range(0, rows, rows // 4)]
    block_copies = []
    for k, (row, size) in enumerate(parts):
        block_copies.append(
            [
                pltpu.make_async_copy(
                    blocks[ref].at[pl.ds(start + row, size), :],
                    block_ref.at[j, pl.ds(row, size), :],
                    block_sem.at[k],
                )
                for j, (ref, start) in enumerate(slots)
            ]
        )
    for copies in block_copies:
        for copy in copies:
            copy.start()
    weight_copies = load_weights(source_ref, weight_ref, sem, strip)
    columns = slot_columns(places_ref, len(slots), width)
    for copy in block_copies[0]:
        copy.wait()
    gains = [
        block_ref[j, pl.ds(rows, GAIN_ROWS), :][:1].astype(jnp.float32) for j in range(len(slots))
    ]

    for k in range(2):
        for copy in block_copies[1 + k]:
            copy.wait()

        def first_step(i, carry):
            normalize(block_ref, gains, columns, k * rows // 4 + i * ROW_TILE, normed_ref)
            return carry

        lax.fori_loop(0, rows // 4 // ROW_TILE, first_step, 0)

    for copies in (block_copies[3], block_copies[4], weight_copies):
        for copy in copies:
            copy.wait()
    steps = half // (2 * ROW_TILE)
    depth = features // steps
    total_ref[...] = jnp.zeros_like(total_ref)

    def second_step(i, carry):
        at = pl.ds(pl.multiple_of(i * depth, depth), depth)
        total_ref[...] += jnp.dot(
            normed_ref[:half, at], weight_ref[at, :], preferred_element_type=jnp.float32
        )
        for k in range(2):
            normalize(block_ref, gains, columns, half + (2 * i + k) * ROW_TILE, normed_ref)
        return carry

    lax.fori_loop(0, steps, second_step, 0)
    sums_ref[:half] = total_ref[...].astype(jnp.bfloat16)
    sums_ref[half:] = jnp.dot(
        normed_ref[half:], weight_ref[...], preferred_element_type=jnp.float32
    ).astype(jnp.bfloat16)
    local = out_ref.shape[1]
    span, window = 128, 256
    for row in range(0, rows, span):
        low = min(max(row - (window - span) // 2, 0), rows - window)
        same = seg_col_ref[row : row + span, :1] == seg_row_ref[:1, low : low + window]
        heads = range(0, local, HEAD_DIM)
        scores = [
            lax.dot_general(
                sums_ref[row : row + span, col : col + HEAD_DIM],
                sums_ref[low : low + window, local + col : local + col + HEAD_DIM],
                (((1,), (1,)), ((), ())),
                preferred_element_type=jnp.float32,
            )
            * (1.0 / math.sqrt(HEAD_DIM))
            for col in heads
        ]
        scores = [jnp.where(same, one, -jnp.inf) for one in scores]
        tops = [jnp.max(one, axis=1, keepdims=True) for one in scores]
        expos = [jnp.exp(one - top) for one, top in zip(scores, tops)]
        shares = [1.0 / jnp.sum(expo, axis=1, keepdims=True) for expo in expos]
        for col, expo, share in zip(heads, expos, shares):
            value = sums_ref[low : low + window, 2 * local + col : 2 * local + col + HEAD_DIM]
            out_ref[row : row + span, col : col + HEAD_DIM] = jnp.dot(
                (expo * share).astype(jnp.bfloat16), value, preferred_element_type=jnp.float32
            ).astype(jnp.bfloat16)


def shards(page_patches, gain, q_weight, k_weight, v_weight, pack_lengths, line_order):
    groups = lax.axis_size("dp")
    page_index = lax.axis_index("dp")
    width = page_patches.shape[1]
    slot_rows = page_patches.shape[0] // groups
    rows = slot_rows * groups // 2
    local = q_weight.shape[1]
    strip = q_weight.shape[0]
    weight = jnp.concatenate([q_weight, k_weight, v_weight], axis=1)
    weight = lax.all_gather(weight, "dp", axis=0, tiled=True, axis_index_groups=dp_groups("z"))
    targets = jnp.arange(groups, dtype=jnp.int32)
    my_order = lax.dynamic_index_in_dim(line_order, page_index, 0, keepdims=False)
    slot_for = jnp.sum(
        jnp.where(my_order[None, :] == targets[:, None], targets[None, :], 0), axis=1
    )
    slots = page_patches.reshape(groups, slot_rows, width)
    outgoing = slots.at[slot_for].get(mode="promise_in_bounds")
    outgoing, pack_lengths = lax.optimization_barrier((outgoing, pack_lengths))
    incoming = lax.all_to_all(outgoing, "dp", split_axis=0, concat_axis=0, tiled=True)
    my_lengths = lax.dynamic_index_in_dim(pack_lengths, page_index, 0, keepdims=False)
    line_ends = jnp.cumsum(my_lengths)
    line_starts = line_ends - my_lengths
    row_ids = jnp.arange(rows, dtype=jnp.int32)
    segment = jnp.sum((line_ends[None, :] <= row_ids[:, None]).astype(jnp.int32), axis=1)
    start_of_row = jnp.sum(
        jnp.where(segment[:, None] == targets[None, :], line_starts[None, :], 0), axis=1
    )
    source_rows = segment * slot_rows + row_ids - start_of_row
    packed = incoming.reshape(groups * slot_rows, width).at[source_rows].get(
        mode="promise_in_bounds"
    )

    own = jnp.concatenate([packed, jnp.broadcast_to(gain[None, :], (GAIN_ROWS, width))], axis=0)
    all_rows = rows + GAIN_ROWS
    cut = rows // 2 + GAIN_ROWS

    def along_y(block, step):
        return lax.ppermute(block, "tensor", y_shift(step))

    def along_z(block, step):
        return lax.ppermute(block, "tensor", z_shift(step))

    z_up, z_down, own_up, own_down, own_far, weight = lax.optimization_barrier(
        (
            along_z(own, 1),
            along_z(own, -1),
            along_y(own, 1),
            along_y(own, -1),
            along_y(own, 2),
            weight,
        )
    )
    weight = lax.all_gather(weight, "dp", axis=0, tiled=True, axis_index_groups=dp_groups("xc"))
    pair = jnp.concatenate([z_up, z_down], axis=0)
    pair_up, pair_down = along_y(pair, 1), along_y(pair, -1)
    pair_far_up = along_y(pair_up[:all_rows], 1)
    pair_far_down = along_y(pair_down[all_rows:], -1)
    far_top, far_rest = along_z(z_up[:cut], 1), along_z(z_down[cut:], -1)
    far = jnp.concatenate([far_top, far_rest], axis=0)
    far_all = lax.all_to_all(
        jnp.broadcast_to(far[None], (Y_PARTS, *far.shape)),
        "tensor",
        split_axis=0,
        concat_axis=0,
        tiled=True,
        axis_index_groups=[[z * Y_PARTS + y for y in range(Y_PARTS)] for z in range(Z_PARTS)],
    )

    blocks, slots_at, shifts = [], [], []

    def add(array, dy, *dzs):
        blocks.append(array)
        for k, dz in enumerate(dzs):
            slots_at.append((len(blocks) - 1, k * all_rows))
            shifts.append((dz, dy))

    add(own, 0, 0)
    add(own_up, -1, 0)
    add(own_down, 1, 0)
    add(own_far, 2, 0)
    add(pair, 0, -1, 1)
    add(pair_up, -1, -1, 1)
    add(pair_down, 1, -1, 1)
    add(pair_far_up, 2, -1)
    add(pair_far_down, 2, 1)
    blocks.append(far_all.reshape(Y_PARTS * all_rows, width))
    for y in range(Y_PARTS):
        slots_at.append((len(blocks) - 1, y * all_rows))
    tensor = lax.axis_index("tensor")
    my_z, my_y = tensor // Y_PARTS, tensor % Y_PARTS
    step_z = jnp.array([dz for dz, _ in shifts] + [2] * Y_PARTS, jnp.int32)
    step_y = jnp.array([dy for _, dy in shifts], jnp.int32)
    step_y = jnp.concatenate([step_y, jnp.arange(Y_PARTS, dtype=jnp.int32) - my_y])
    places = (my_z + step_z + Z_PARTS) % Z_PARTS * Y_PARTS + (my_y + step_y + Y_PARTS) % Y_PARTS

    def kernel(*refs):
        project_attend_kernel(slots_at, len(blocks), rows, strip, *refs)

    features = width * len(slots_at)
    vmem = pl.BlockSpec(memory_space=pltpu.VMEM)
    smem, hbm = pl.BlockSpec(memory_space=pltpu.SMEM), pl.BlockSpec(memory_space=pl.ANY)
    return pl.pallas_call(
        kernel,
        out_shape=jax.ShapeDtypeStruct((rows, local), jnp.bfloat16),
        in_specs=[smem] + [hbm] * (len(blocks) + 1) + [vmem, vmem],
        out_specs=vmem,
        scratch_shapes=[
            pltpu.VMEM((len(slots_at), all_rows, width), jnp.bfloat16),
            pltpu.VMEM((rows, features), jnp.bfloat16),
            pltpu.VMEM((features, 3 * local), jnp.bfloat16),
            pltpu.VMEM((rows // 2, 3 * local), jnp.float32),
            pltpu.VMEM((rows, 3 * local), jnp.bfloat16),
            pltpu.SemaphoreType.DMA,
            pltpu.SemaphoreType.DMA((5,)),
        ],
        name="norm_project_attend",
    )(places, *blocks, weight, segment[:, None], segment[None, :])


def solution(mesh):
    return jax.shard_map(
        shards,
        mesh=mesh,
        in_specs=(
            P("dp", "tensor"),
            P("tensor"),
            P("dp", "tensor"),
            P("dp", "tensor"),
            P("dp", "tensor"),
            P(),
            P(),
        ),
        out_specs=P("dp", "tensor"),
        check_vma=False,
    )
```

```python
import math

import jax
import jax.numpy as jnp
from jax import lax
from jax.experimental import pallas as pl
from jax.experimental.pallas import tpu as pltpu
from jax.sharding import PartitionSpec as P

HEAD_DIM = 128
NORM_EPSILON = 1e-06
Z_PARTS, Y_PARTS = 4, 4
GAIN_ROWS = 16
ROW_TILE = 16


def z_shift(step):
    return [
        (z * Y_PARTS + y, (z + step) % Z_PARTS * Y_PARTS + y)
        for z in range(Z_PARTS)
        for y in range(Y_PARTS)
    ]


def y_shift(step):
    return [
        (z * Y_PARTS + y, z * Y_PARTS + (y + step) % Y_PARTS)
        for z in range(Z_PARTS)
        for y in range(Y_PARTS)
    ]


def dp_groups(varying):
    groups = {}
    for x in range(4):
        for z in range(4):
            for core in range(2):
                key = tuple(v for name, v in (("x", x), ("z", z), ("c", core)) if name not in varying)
                groups.setdefault(key, []).append(x * 8 + z * 2 + core)
    return list(groups.values())


def load_weights(source_ref, weight_ref, sem, strip):
    copies = []
    for x in range(4):
        for z in range(4):
            for core in range(2):
                held, wanted = (x * 2 + core) * 4 + z, x * 8 + z * 2 + core
                copies.append(
                    pltpu.make_async_copy(
                        source_ref.at[pl.ds(held * strip, strip), :],
                        weight_ref.at[pl.ds(wanted * strip, strip), :],
                        sem,
                    )
                )
    for copy in copies:
        copy.start()
    return copies


def slot_columns(places_ref, count, width):
    return [pl.ds(pl.multiple_of(places_ref[j] * width, 128), width) for j in range(count)]


def normalize(block_ref, gains, columns, row, normed_ref):
    features = normed_ref.shape[1]
    at = pl.multiple_of(row, ROW_TILE)

    def load(j):
        return block_ref[j, pl.ds(at, ROW_TILE), :].astype(jnp.float32)

    total = load(0)
    for j in range(1, len(gains)):
        total = total + load(j)
    mean = jnp.sum(total, axis=1, keepdims=True) * (1.0 / features)
    square = jnp.square(load(0) - mean)
    for j in range(1, len(gains)):
        square = square + jnp.square(load(j) - mean)
    var = jnp.sum(square, axis=1, keepdims=True) * (1.0 / features)
    scale = lax.rsqrt(var + NORM_EPSILON)
    for j in range(len(gains)):
        normed_ref[pl.ds(at, ROW_TILE), columns[j]] = (
            (load(j) - mean) * scale * gains[j]
        ).astype(jnp.bfloat16)


def project_attend_kernel(slots, count, rows, strip, *refs):
    places_ref, blocks = refs[0], refs[1 : 1 + count]
    source_ref, seg_col_ref, seg_row_ref, out_ref = refs[1 + count : 5 + count]
    block_ref, normed_ref, weight_ref, total_ref, sums_ref, sem, block_sem = refs[5 + count :]
    width, features = block_ref.shape[2], normed_ref.shape[1]
    half = rows // 2
    parts = [(rows, GAIN_ROWS)] + [(row, rows // 4) for row in range(0, rows, rows // 4)]
    block_copies = []
    for k, (row, size) in enumerate(parts):
        block_copies.append(
            [
                pltpu.make_async_copy(
                    blocks[ref].at[pl.ds(start + row, size), :],
                    block_ref.at[j, pl.ds(row, size), :],
                    block_sem.at[k],
                )
                for j, (ref, start) in enumerate(slots)
            ]
        )
    for copies in block_copies:
        for copy in copies:
            copy.start()
    weight_copies = load_weights(source_ref, weight_ref, sem, strip)
    columns = slot_columns(places_ref, len(slots), width)
    for copy in block_copies[0]:
        copy.wait()
    gains = [
        block_ref[j, pl.ds(rows, GAIN_ROWS), :][:1].astype(jnp.float32) for j in range(len(slots))
    ]

    for k in range(2):
        for copy in block_copies[1 + k]:
            copy.wait()

        def first_step(i, carry):
            normalize(block_ref, gains, columns, k * rows // 4 + i * ROW_TILE, normed_ref)
            return carry

        lax.fori_loop(0, rows // 4 // ROW_TILE, first_step, 0)

    for copies in (block_copies[3], block_copies[4], weight_copies):
        for copy in copies:
            copy.wait()
    steps = half // (2 * ROW_TILE)
    depth = features // steps
    total_ref[...] = jnp.zeros_like(total_ref)

    def second_step(i, carry):
        at = pl.ds(pl.multiple_of(i * depth, depth), depth)
        total_ref[...] += jnp.dot(
            normed_ref[:half, at], weight_ref[at, :], preferred_element_type=jnp.float32
        )
        for k in range(2):
            normalize(block_ref, gains, columns, half + (2 * i + k) * ROW_TILE, normed_ref)
        return carry

    lax.fori_loop(0, steps, second_step, 0)
    sums_ref[:half] = total_ref[...].astype(jnp.bfloat16)
    sums_ref[half:] = jnp.dot(
        normed_ref[half:], weight_ref[...], preferred_element_type=jnp.float32
    ).astype(jnp.bfloat16)
    local = out_ref.shape[1]
    span, window = 128, 256
    for start in range(0, rows, 2 * span):
        units = []
        for row in (start, start + span):
            low = min(max(row - (window - span) // 2, 0), rows - window)
            same = seg_col_ref[row : row + span, :1] == seg_row_ref[:1, low : low + window]
            units += [(row, low, same, col) for col in range(0, local, HEAD_DIM)]
        scores = [
            lax.dot_general(
                sums_ref[row : row + span, col : col + HEAD_DIM],
                sums_ref[low : low + window, local + col : local + col + HEAD_DIM],
                (((1,), (1,)), ((), ())),
                preferred_element_type=jnp.float32,
            )
            * (1.0 / math.sqrt(HEAD_DIM))
            for row, low, _, col in units
        ]
        scores = [jnp.where(unit[2], one, -jnp.inf) for unit, one in zip(units, scores)]
        tops = [jnp.max(one, axis=1, keepdims=True) for one in scores]
        expos = [jnp.exp(one - top) for one, top in zip(scores, tops)]
        shares = [1.0 / jnp.sum(expo, axis=1, keepdims=True) for expo in expos]
        for (row, low, _, col), expo, share in zip(units, expos, shares):
            value = sums_ref[low : low + window, 2 * local + col : 2 * local + col + HEAD_DIM]
            out_ref[row : row + span, col : col + HEAD_DIM] = jnp.dot(
                (expo * share).astype(jnp.bfloat16), value, preferred_element_type=jnp.float32
            ).astype(jnp.bfloat16)


def shards(page_patches, gain, q_weight, k_weight, v_weight, pack_lengths, line_order):
    groups = lax.axis_size("dp")
    page_index = lax.axis_index("dp")
    width = page_patches.shape[1]
    slot_rows = page_patches.shape[0] // groups
    rows = slot_rows * groups // 2
    local = q_weight.shape[1]
    strip = q_weight.shape[0]
    weight = jnp.concatenate([q_weight, k_weight, v_weight], axis=1)
    weight = lax.all_gather(weight, "dp", axis=0, tiled=True, axis_index_groups=dp_groups("z"))
    targets = jnp.arange(groups, dtype=jnp.int32)
    my_order = lax.dynamic_index_in_dim(line_order, page_index, 0, keepdims=False)
    slot_for = jnp.sum(
        jnp.where(my_order[None, :] == targets[:, None], targets[None, :], 0), axis=1
    )
    slots = page_patches.reshape(groups, slot_rows, width)
    outgoing = slots.at[slot_for].get(mode="promise_in_bounds")
    outgoing, pack_lengths = lax.optimization_barrier((outgoing, pack_lengths))
    incoming = lax.all_to_all(outgoing, "dp", split_axis=0, concat_axis=0, tiled=True)
    my_lengths = lax.dynamic_index_in_dim(pack_lengths, page_index, 0, keepdims=False)
    line_ends = jnp.cumsum(my_lengths)
    line_starts = line_ends - my_lengths
    row_ids = jnp.arange(rows, dtype=jnp.int32)
    segment = jnp.sum((line_ends[None, :] <= row_ids[:, None]).astype(jnp.int32), axis=1)
    start_of_row = jnp.sum(
        jnp.where(segment[:, None] == targets[None, :], line_starts[None, :], 0), axis=1
    )
    source_rows = segment * slot_rows + row_ids - start_of_row
    packed = incoming.reshape(groups * slot_rows, width).at[source_rows].get(
        mode="promise_in_bounds"
    )

    own = jnp.concatenate([packed, jnp.broadcast_to(gain[None, :], (GAIN_ROWS, width))], axis=0)
    all_rows = rows + GAIN_ROWS
    cut = rows // 2 + GAIN_ROWS

    def along_y(block, step):
        return lax.ppermute(block, "tensor", y_shift(step))

    def along_z(block, step):
        return lax.ppermute(block, "tensor", z_shift(step))

    z_up, z_down, own_up, own_down, own_far, weight = lax.optimization_barrier(
        (
            along_z(own, 1),
            along_z(own, -1),
            along_y(own, 1),
            along_y(own, -1),
            along_y(own, 2),
            weight,
        )
    )
    weight = lax.all_gather(weight, "dp", axis=0, tiled=True, axis_index_groups=dp_groups("xc"))
    pair = jnp.concatenate([z_up, z_down], axis=0)
    pair_up, pair_down = along_y(pair, 1), along_y(pair, -1)
    pair_far_up = along_y(pair_up[:all_rows], 1)
    pair_far_down = along_y(pair_down[all_rows:], -1)
    far_top, far_rest = along_z(z_up[:cut], 1), along_z(z_down[cut:], -1)
    far = jnp.concatenate([far_top, far_rest], axis=0)
    far_all = lax.all_to_all(
        jnp.broadcast_to(far[None], (Y_PARTS, *far.shape)),
        "tensor",
        split_axis=0,
        concat_axis=0,
        tiled=True,
        axis_index_groups=[[z * Y_PARTS + y for y in range(Y_PARTS)] for z in range(Z_PARTS)],
    )

    blocks, slots_at, shifts = [], [], []

    def add(array, dy, *dzs):
        blocks.append(array)
        for k, dz in enumerate(dzs):
            slots_at.append((len(blocks) - 1, k * all_rows))
            shifts.append((dz, dy))

    add(own, 0, 0)
    add(own_up, -1, 0)
    add(own_down, 1, 0)
    add(own_far, 2, 0)
    add(pair, 0, -1, 1)
    add(pair_up, -1, -1, 1)
    add(pair_down, 1, -1, 1)
    add(pair_far_up, 2, -1)
    add(pair_far_down, 2, 1)
    blocks.append(far_all.reshape(Y_PARTS * all_rows, width))
    for y in range(Y_PARTS):
        slots_at.append((len(blocks) - 1, y * all_rows))
    tensor = lax.axis_index("tensor")
    my_z, my_y = tensor // Y_PARTS, tensor % Y_PARTS
    step_z = jnp.array([dz for dz, _ in shifts] + [2] * Y_PARTS, jnp.int32)
    step_y = jnp.array([dy for _, dy in shifts], jnp.int32)
    step_y = jnp.concatenate([step_y, jnp.arange(Y_PARTS, dtype=jnp.int32) - my_y])
    places = (my_z + step_z + Z_PARTS) % Z_PARTS * Y_PARTS + (my_y + step_y + Y_PARTS) % Y_PARTS

    def kernel(*refs):
        project_attend_kernel(slots_at, len(blocks), rows, strip, *refs)

    features = width * len(slots_at)
    vmem = pl.BlockSpec(memory_space=pltpu.VMEM)
    smem, hbm = pl.BlockSpec(memory_space=pltpu.SMEM), pl.BlockSpec(memory_space=pl.ANY)
    return pl.pallas_call(
        kernel,
        out_shape=jax.ShapeDtypeStruct((rows, local), jnp.bfloat16),
        in_specs=[smem] + [hbm] * (len(blocks) + 1) + [vmem, vmem],
        out_specs=vmem,
        scratch_shapes=[
            pltpu.VMEM((len(slots_at), all_rows, width), jnp.bfloat16),
            pltpu.VMEM((rows, features), jnp.bfloat16),
            pltpu.VMEM((features, 3 * local), jnp.bfloat16),
            pltpu.VMEM((rows // 2, 3 * local), jnp.float32),
            pltpu.VMEM((rows, 3 * local), jnp.bfloat16),
            pltpu.SemaphoreType.DMA,
            pltpu.SemaphoreType.DMA((5,)),
        ],
        name="norm_project_attend",
    )(places, *blocks, weight, segment[:, None], segment[None, :])


def solution(mesh):
    return jax.shard_map(
        shards,
        mesh=mesh,
        in_specs=(
            P("dp", "tensor"),
            P("tensor"),
            P("dp", "tensor"),
            P("dp", "tensor"),
            P("dp", "tensor"),
            P(),
            P(),
        ),
        out_specs=P("dp", "tensor"),
        check_vma=False,
    )
```

```python
import math

import jax
import jax.numpy as jnp
from jax import lax
from jax.experimental import pallas as pl
from jax.experimental.pallas import tpu as pltpu
from jax.sharding import PartitionSpec as P

HEAD_DIM = 128
NORM_EPSILON = 1e-06
Z_PARTS, Y_PARTS = 4, 4
GAIN_ROWS = 16
ROW_TILE = 16


def z_shift(step):
    return [
        (z * Y_PARTS + y, (z + step) % Z_PARTS * Y_PARTS + y)
        for z in range(Z_PARTS)
        for y in range(Y_PARTS)
    ]


def y_shift(step):
    return [
        (z * Y_PARTS + y, z * Y_PARTS + (y + step) % Y_PARTS)
        for z in range(Z_PARTS)
        for y in range(Y_PARTS)
    ]


def dp_groups(varying):
    groups = {}
    for x in range(4):
        for z in range(4):
            for core in range(2):
                key = tuple(v for name, v in (("x", x), ("z", z), ("c", core)) if name not in varying)
                groups.setdefault(key, []).append(x * 8 + z * 2 + core)
    return list(groups.values())


def load_weights(source_ref, weight_ref, sem, strip):
    copies = []
    for x in range(4):
        for z in range(4):
            for core in range(2):
                held, wanted = (x * 2 + core) * 4 + z, x * 8 + z * 2 + core
                copies.append(
                    pltpu.make_async_copy(
                        source_ref.at[pl.ds(held * strip, strip), :],
                        weight_ref.at[pl.ds(wanted * strip, strip), :],
                        sem,
                    )
                )
    for copy in copies:
        copy.start()
    return copies


def slot_columns(places_ref, count, width):
    return [pl.ds(pl.multiple_of(places_ref[j] * width, 128), width) for j in range(count)]


def normalize(block_ref, gains, columns, row, normed_ref):
    features = normed_ref.shape[1]
    at = pl.multiple_of(row, ROW_TILE)

    def load(j):
        return block_ref[j, pl.ds(at, ROW_TILE), :].astype(jnp.float32)

    total = load(0)
    for j in range(1, len(gains)):
        total = total + load(j)
    mean = jnp.sum(total, axis=1, keepdims=True) * (1.0 / features)
    square = jnp.square(load(0) - mean)
    for j in range(1, len(gains)):
        square = square + jnp.square(load(j) - mean)
    var = jnp.sum(square, axis=1, keepdims=True) * (1.0 / features)
    scale = lax.rsqrt(var + NORM_EPSILON)
    for j in range(len(gains)):
        normed_ref[pl.ds(at, ROW_TILE), columns[j]] = (
            (load(j) - mean) * scale * gains[j]
        ).astype(jnp.bfloat16)


def project_attend_kernel(slots, count, rows, strip, *refs):
    places_ref, blocks = refs[0], refs[1 : 1 + count]
    source_ref, seg_col_ref, seg_row_ref, out_ref = refs[1 + count : 5 + count]
    block_ref, normed_ref, weight_ref, total_ref, sums_ref, sem, block_sem = refs[5 + count :]
    width, features = block_ref.shape[2], normed_ref.shape[1]
    half = rows // 2
    parts = [(rows, GAIN_ROWS)] + [(row, rows // 4) for row in range(0, rows, rows // 4)]
    block_copies = []
    for k, (row, size) in enumerate(parts):
        block_copies.append(
            [
                pltpu.make_async_copy(
                    blocks[ref].at[pl.ds(start + row, size), :],
                    block_ref.at[j, pl.ds(row, size), :],
                    block_sem.at[k],
                )
                for j, (ref, start) in enumerate(slots)
            ]
        )
    for copies in block_copies:
        for copy in copies:
            copy.start()
    weight_copies = load_weights(source_ref, weight_ref, sem, strip)
    columns = slot_columns(places_ref, len(slots), width)
    for copy in block_copies[0]:
        copy.wait()
    gains = [
        block_ref[j, pl.ds(rows, GAIN_ROWS), :][:1].astype(jnp.float32) for j in range(len(slots))
    ]

    for k in range(2):
        for copy in block_copies[1 + k]:
            copy.wait()

        def first_step(i, carry):
            normalize(block_ref, gains, columns, k * rows // 4 + i * ROW_TILE, normed_ref)
            return carry

        lax.fori_loop(0, rows // 4 // ROW_TILE, first_step, 0)

    for copies in (block_copies[3], block_copies[4], weight_copies):
        for copy in copies:
            copy.wait()
    steps = half // (2 * ROW_TILE)
    depth = features // steps
    total_ref[...] = jnp.zeros_like(total_ref)

    def second_step(i, carry):
        at = pl.ds(pl.multiple_of(i * depth, depth), depth)
        total_ref[...] += jnp.dot(
            normed_ref[:half, at], weight_ref[at, :], preferred_element_type=jnp.float32
        )
        for k in range(2):
            normalize(block_ref, gains, columns, half + (2 * i + k) * ROW_TILE, normed_ref)
        return carry

    lax.fori_loop(0, steps, second_step, 0)
    sums_ref[:half] = total_ref[...].astype(jnp.bfloat16)
    sums_ref[half:] = jnp.dot(
        normed_ref[half:], weight_ref[...], preferred_element_type=jnp.float32
    ).astype(jnp.bfloat16)
    local = out_ref.shape[1]
    span, window = 128, 256
    for start in range(0, rows, 4 * span):
        units = []
        for row in range(start, start + 4 * span, span):
            low = min(max(row - (window - span) // 2, 0), rows - window)
            same = seg_col_ref[row : row + span, :1] == seg_row_ref[:1, low : low + window]
            units += [(row, low, same, col) for col in range(0, local, HEAD_DIM)]
        scores = [
            lax.dot_general(
                sums_ref[row : row + span, col : col + HEAD_DIM],
                sums_ref[low : low + window, local + col : local + col + HEAD_DIM],
                (((1,), (1,)), ((), ())),
                preferred_element_type=jnp.float32,
            )
            * (1.0 / math.sqrt(HEAD_DIM))
            for row, low, _, col in units
        ]
        scores = [jnp.where(unit[2], one, -jnp.inf) for unit, one in zip(units, scores)]
        tops = [jnp.max(one, axis=1, keepdims=True) for one in scores]
        expos = [jnp.exp(one - top) for one, top in zip(scores, tops)]
        shares = [1.0 / jnp.sum(expo, axis=1, keepdims=True) for expo in expos]
        for (row, low, _, col), expo, share in zip(units, expos, shares):
            value = sums_ref[low : low + window, 2 * local + col : 2 * local + col + HEAD_DIM]
            out_ref[row : row + span, col : col + HEAD_DIM] = jnp.dot(
                (expo * share).astype(jnp.bfloat16), value, preferred_element_type=jnp.float32
            ).astype(jnp.bfloat16)


def shards(page_patches, gain, q_weight, k_weight, v_weight, pack_lengths, line_order):
    groups = lax.axis_size("dp")
    page_index = lax.axis_index("dp")
    width = page_patches.shape[1]
    slot_rows = page_patches.shape[0] // groups
    rows = slot_rows * groups // 2
    local = q_weight.shape[1]
    strip = q_weight.shape[0]
    weight = jnp.concatenate([q_weight, k_weight, v_weight], axis=1)
    weight = lax.all_gather(weight, "dp", axis=0, tiled=True, axis_index_groups=dp_groups("z"))
    targets = jnp.arange(groups, dtype=jnp.int32)
    my_order = lax.dynamic_index_in_dim(line_order, page_index, 0, keepdims=False)
    slot_for = jnp.sum(
        jnp.where(my_order[None, :] == targets[:, None], targets[None, :], 0), axis=1
    )
    slots = page_patches.reshape(groups, slot_rows, width)
    outgoing = slots.at[slot_for].get(mode="promise_in_bounds")
    outgoing, pack_lengths = lax.optimization_barrier((outgoing, pack_lengths))
    incoming = lax.all_to_all(outgoing, "dp", split_axis=0, concat_axis=0, tiled=True)
    my_lengths = lax.dynamic_index_in_dim(pack_lengths, page_index, 0, keepdims=False)
    line_ends = jnp.cumsum(my_lengths)
    line_starts = line_ends - my_lengths
    row_ids = jnp.arange(rows, dtype=jnp.int32)
    segment = jnp.sum((line_ends[None, :] <= row_ids[:, None]).astype(jnp.int32), axis=1)
    start_of_row = jnp.sum(
        jnp.where(segment[:, None] == targets[None, :], line_starts[None, :], 0), axis=1
    )
    source_rows = segment * slot_rows + row_ids - start_of_row
    packed = incoming.reshape(groups * slot_rows, width).at[source_rows].get(
        mode="promise_in_bounds"
    )

    own = jnp.concatenate([packed, jnp.broadcast_to(gain[None, :], (GAIN_ROWS, width))], axis=0)
    all_rows = rows + GAIN_ROWS
    cut = rows // 2 + GAIN_ROWS

    def along_y(block, step):
        return lax.ppermute(block, "tensor", y_shift(step))

    def along_z(block, step):
        return lax.ppermute(block, "tensor", z_shift(step))

    z_up, z_down, own_up, own_down, own_far, weight = lax.optimization_barrier(
        (
            along_z(own, 1),
            along_z(own, -1),
            along_y(own, 1),
            along_y(own, -1),
            along_y(own, 2),
            weight,
        )
    )
    weight = lax.all_gather(weight, "dp", axis=0, tiled=True, axis_index_groups=dp_groups("xc"))
    pair = jnp.concatenate([z_up, z_down], axis=0)
    pair_up, pair_down = along_y(pair, 1), along_y(pair, -1)
    pair_far_up = along_y(pair_up[:all_rows], 1)
    pair_far_down = along_y(pair_down[all_rows:], -1)
    far_top, far_rest = along_z(z_up[:cut], 1), along_z(z_down[cut:], -1)
    far = jnp.concatenate([far_top, far_rest], axis=0)
    far_all = lax.all_to_all(
        jnp.broadcast_to(far[None], (Y_PARTS, *far.shape)),
        "tensor",
        split_axis=0,
        concat_axis=0,
        tiled=True,
        axis_index_groups=[[z * Y_PARTS + y for y in range(Y_PARTS)] for z in range(Z_PARTS)],
    )

    blocks, slots_at, shifts = [], [], []

    def add(array, dy, *dzs):
        blocks.append(array)
        for k, dz in enumerate(dzs):
            slots_at.append((len(blocks) - 1, k * all_rows))
            shifts.append((dz, dy))

    add(own, 0, 0)
    add(own_up, -1, 0)
    add(own_down, 1, 0)
    add(own_far, 2, 0)
    add(pair, 0, -1, 1)
    add(pair_up, -1, -1, 1)
    add(pair_down, 1, -1, 1)
    add(pair_far_up, 2, -1)
    add(pair_far_down, 2, 1)
    blocks.append(far_all.reshape(Y_PARTS * all_rows, width))
    for y in range(Y_PARTS):
        slots_at.append((len(blocks) - 1, y * all_rows))
    tensor = lax.axis_index("tensor")
    my_z, my_y = tensor // Y_PARTS, tensor % Y_PARTS
    step_z = jnp.array([dz for dz, _ in shifts] + [2] * Y_PARTS, jnp.int32)
    step_y = jnp.array([dy for _, dy in shifts], jnp.int32)
    step_y = jnp.concatenate([step_y, jnp.arange(Y_PARTS, dtype=jnp.int32) - my_y])
    places = (my_z + step_z + Z_PARTS) % Z_PARTS * Y_PARTS + (my_y + step_y + Y_PARTS) % Y_PARTS

    def kernel(*refs):
        project_attend_kernel(slots_at, len(blocks), rows, strip, *refs)

    features = width * len(slots_at)
    vmem = pl.BlockSpec(memory_space=pltpu.VMEM)
    smem, hbm = pl.BlockSpec(memory_space=pltpu.SMEM), pl.BlockSpec(memory_space=pl.ANY)
    return pl.pallas_call(
        kernel,
        out_shape=jax.ShapeDtypeStruct((rows, local), jnp.bfloat16),
        in_specs=[smem] + [hbm] * (len(blocks) + 1) + [vmem, vmem],
        out_specs=vmem,
        scratch_shapes=[
            pltpu.VMEM((len(slots_at), all_rows, width), jnp.bfloat16),
            pltpu.VMEM((rows, features), jnp.bfloat16),
            pltpu.VMEM((features, 3 * local), jnp.bfloat16),
            pltpu.VMEM((rows // 2, 3 * local), jnp.float32),
            pltpu.VMEM((rows, 3 * local), jnp.bfloat16),
            pltpu.SemaphoreType.DMA,
            pltpu.SemaphoreType.DMA((5,)),
        ],
        name="norm_project_attend",
    )(places, *blocks, weight, segment[:, None], segment[None, :])


def solution(mesh):
    return jax.shard_map(
        shards,
        mesh=mesh,
        in_specs=(
            P("dp", "tensor"),
            P("tensor"),
            P("dp", "tensor"),
            P("dp", "tensor"),
            P("dp", "tensor"),
            P(),
            P(),
        ),
        out_specs=P("dp", "tensor"),
        check_vma=False,
    )
```
